512 devices in a mesh: head: 16 (over y, x), tok: 32 (over z, core).
Axes of the slice: x: 4, y: 4, z: 16, core: 2. Of those that a mesh axis runs over, the one named last changes fastest.
Arguments:
- stretch_tokens: bfloat16 [32, 1024, 1792], P('tok', 'head'), may hold values from -6 to 6
- stretch_tail: bfloat16 [32, 2, 1792], P('tok'), may hold values from -6 to 6
- decode_tokens: bfloat16 [32, 32, 1792], P('tok'), may hold values from -6 to 6
- decode_tail: bfloat16 [32, 32, 2, 1792], P('tok'), may hold values from -6 to 6
- norm_gain: float32 [1792], replicated, may hold values from 0.1 to 1.9
- conv_taps: float32 [3, 1792], replicated, may hold values from -3 to 3
- qkv_weight: bfloat16 [1792, 16, 144], P(None, 'head'), may hold values from -0.125 to 0.125
- out_gain: float32 [1792], P('head'), may hold values from 0.1 to 1.9
- out_weight: bfloat16 [1792, 1792], P('head'), may hold values from -0.125 to 0.125
- state_cache: float32 [32, 16, 16, 112, 273], P('tok', None, 'head'), may hold values from -24 to 24
- stretch_len: int32 [32], P('tok'), may hold values from 1 to 1024, 16384 in all
- stretch_slot: int32 [32], P('tok'), may hold values from 0 to 15
- decode_slot: int32 [32, 32], P('tok'), may hold values from 0 to 15
- decode_owner: int32 [32, 32, 1], P('tok'), may hold values from 0 to 31; in each aligned block of 32 rows (0 to 31, 32 to 63, ..., all dimensions but the last counted through in order) at most 2 rows name the same one
Outputs:
- stretch_out: bfloat16 [32, 1024, 1792], P('tok', 'head')
- decode_out: bfloat16 [32, 32, 1792], P('tok', 'head')
- state_new: float32 [32, 16, 112, 273], P('tok', 'head')
The draws below stay inside these ranges and needn't reach their ends.
Inputs may be any that keep to these rules, and one draw needn't show every extreme that they name: `decode_owner`: in the 32 decoders of one group at most 2 name the same owner group, a bound that some block reaches of them. `stretch_len`: some group's stretch is full.
All inputs are finite; a program needn't handle non-finite values.
Results may differ from the reference program's by a relative error of at most 0.014.
Values may be sent and summed in bfloat16 or wider, within the bound.
A program may use at most 64 MiB of HBM per device.

```python
import math
import jax
import jax.numpy as jnp
import numpy as np
from jax import lax

D = 1792
H = 16
DH = 112
F = 16
PHI = 273
STRETCH = 1024
DEC = 32
SLOTS = 16
GROUPS = 32
CAP = 2
N_HEAD = 16


def plant(values, rng, low, high):
    spot = [jax.random.randint(jax.random.fold_in(rng, axis), (), 0, length) for axis, length in enumerate(values.shape)]
    longest = values.shape.index(max(values.shape))
    next_to = spot[:longest] + [(spot[longest] + 1) % values.shape[longest]] + spot[longest + 1:]
    return values.at[tuple(spot)].set(low).at[tuple(next_to)].set(high)


def steps_of(stream_key, extent, split, least, high):
    level, own = 1.0, jax.random.fold_in(stream_key, 6)
    for dim, shards_of in split:
        steps = jnp.exp(jax.random.uniform(jax.random.fold_in(own, dim), (shards_of,), jnp.float32, least / len(split), high / len(split)))
        level = level * jnp.repeat(steps, extent[dim] // shards_of).reshape([-1 if axis == dim else 1 for axis in range(len(extent))])
    return level


def split_up(amount, total, reach, slope):
    weights = [(1 << 20) // math.isqrt(rank ** slope) + 1 for rank in range(2, amount + 1)]
    rest, counts = total - reach - (amount - 1), [1] * (amount - 1)
    while rest > 0:
        free = [i for i in range(amount - 1) if counts[i] < reach]
        pool, left = sum([weights[i] for i in free]), rest
        for i in free:
            addition = min(reach - counts[i], max(1, left * weights[i] // pool), rest)
            counts[i] = counts[i] + addition
            rest = rest - addition
    return np.array([reach] + counts)


def ragged(rng, count, total, limit, skew):
    if count == 2:
        one = jax.random.randint(rng, (), max(1, total - limit), min(limit, total - 1) + 1)
        return jnp.stack([one, total - one])
    tallies = jnp.asarray(split_up(count, total, limit, skew), jnp.int32)
    pairs = (count - 1) // 2
    giver, receiver = tallies[1:1 + 2 * pairs:2], tallies[2:2 + 2 * pairs:2]
    room = jnp.minimum(giver - 1, limit - receiver)
    shifted = jax.random.randint(jax.random.fold_in(rng, 1), (pairs,), 0, 1 << 20) % (room + 1)
    tallies = tallies.at[1:1 + 2 * pairs:2].set(giver - shifted).at[2:2 + 2 * pairs:2].set(receiver + shifted)
    return tallies[jax.random.permutation(jax.random.fold_in(rng, 2), count)]


def deal_out(stream_key, own, number, rows, number_of, top, limit, skew):
    sequence = jax.random.permutation(stream_key, number_of)
    heavy_load, usual = load_shares(number_of, rows * top, limit, skew, True), load_shares(number_of, rows * top, limit, skew, False)
    places = jnp.arange(number_of)

    def named(lengths, rotation):
        used = int((lengths > 0).sum())
        fixed = max(1, used // 4)
        passed = fixed + (places - fixed + rotation * (used - fixed)) % max(1, number_of - fixed)
        return jnp.zeros((number_of,), jnp.int32).at[sequence[jnp.where(places < fixed, places, passed)]].set(jnp.asarray(lengths, jnp.int32))

    lengths = jnp.where(number % 4 == 0, named(heavy_load, number // 4), named(usual, number - number // 4 - 1))
    mixed = jax.random.permutation(jax.random.fold_in(own, 3), number_of)
    source_of, sink = mixed[0:number_of // 2 * 2:2], mixed[1:number_of // 2 * 2:2]
    slack = jnp.minimum(lengths[source_of] - 1, limit - lengths[sink]) // 2
    slack = jnp.where((source_of == sequence[0]) | (sink == sequence[0]) | (lengths[sink] == 0), 0, jnp.maximum(slack, 0))
    passed = jax.random.randint(jax.random.fold_in(own, 4), (number_of // 2,), 0, 1 << 20) % (slack + 1)
    lengths = lengths.at[source_of].add(-passed).at[sink].add(passed)
    labels = jnp.searchsorted(jnp.cumsum(lengths), jnp.arange(rows * top), side="right").astype(jnp.int32)
    listing = labels.reshape(top, rows).T
    listing = listing[jax.random.permutation(jax.random.fold_in(own, 1), rows)]
    rotation = jax.random.randint(jax.random.fold_in(own, 2), (rows, 1), 0, top)
    return jnp.take_along_axis(listing, (jnp.arange(top)[None, :] + rotation) % top, axis=1)


def load_shares(count, total, most, lean, full):
    weights = [(1 << 20) // math.isqrt(standing ** lean) + 1 for standing in range(1, count + 1)]
    largest = most if full else min(most, max(-(-total // count), total * weights[0] // sum(weights)))
    least = 1 if total - largest >= count - 1 else 0
    given, spare = [largest] + [least] * (count - 1), total - largest - least * (count - 1)
    while spare > 0:
        candidates = [i for i in range(1, count) if given[i] < largest] or [i for i in range(1, count) if given[i] < most]
        pool, remaining = sum([weights[i] for i in candidates]), spare
        for i in candidates:
            more = min(most - given[i], max(1, remaining * weights[i] // pool), spare)
            given[i] = given[i] + more
            spare = spare - more
    return np.array(given)


def centred(key, dims, spread, most, split=(), kind=jnp.bfloat16):
    entries = jax.random.normal(key, dims, jnp.float32) * spread
    if len(split) > 0:
        entries = steps_of(key, dims, split, -0.22, 0.18) * entries
    return jnp.clip(entries, min=-most, max=most).astype(kind)


def setup_inputs(seed: int = 0) -> dict:
    arg_keys = jax.random.split(jax.random.key(seed), 15)
    stretch_tokens = centred(arg_keys[0], (GROUPS, STRETCH, D), 1.0, 6.0, ((0, 32), (1, 16)))
    stretch_tail = centred(arg_keys[1], (GROUPS, 2, D), 1.0, 6.0, ((0, 32),))
    decode_tokens = centred(arg_keys[2], (GROUPS, DEC, D), 1.0, 6.0, ((0, 32),))
    decode_tail = centred(arg_keys[3], (GROUPS, DEC, 2, D), 1.0, 6.0, ((0, 32),))
    norm_gain = jnp.clip(1.0 + 0.18 * jax.random.normal(arg_keys[4], (D,), jnp.float32), 0.1, 1.9)
    conv_taps = centred(arg_keys[5], (3, D), 0.6, 3.0, (), jnp.float32)
    qkv_weight = centred(arg_keys[6], (D, H, 2 * F + DH), D ** -0.5, 0.125, ((1, 16),))
    out_gain = jnp.clip(1.0 + 0.18 * jax.random.normal(arg_keys[7], (H * DH,), jnp.float32), 0.1, 1.9)
    out_weight = centred(arg_keys[8], (H * DH, D), (H * DH) ** -0.5, 0.125, ((0, 16),))
    state_cache = centred(arg_keys[9], (GROUPS, SLOTS, H, DH, PHI), 4.0, 24.0, ((0, 32), (2, 16)), jnp.float32)
    stretch_len = ragged(arg_keys[10], GROUPS, GROUPS * STRETCH // 2, STRETCH, 2).astype(jnp.int32)
    stretch_slot = plant(jax.random.randint(arg_keys[11], (GROUPS,), 0, SLOTS), jax.random.fold_in(arg_keys[11], 1), 0, SLOTS - 1).astype(jnp.int32)
    decode_slot = plant(jax.random.randint(arg_keys[12], (GROUPS, DEC), 0, SLOTS), jax.random.fold_in(arg_keys[12], 1), 0, SLOTS - 1).astype(jnp.int32)
    decode_owner_keys = jax.random.split(jax.random.fold_in(arg_keys[13], 1), GROUPS * DEC // DEC)
    decode_owner_turns = jax.random.permutation(jax.random.fold_in(arg_keys[13], 3), GROUPS * DEC // DEC)
    decode_owner = jax.vmap(lambda own, number: deal_out(jax.random.fold_in(arg_keys[13], 2), own, number, DEC, GROUPS, 1, CAP, 2))(decode_owner_keys, decode_owner_turns).reshape((GROUPS, DEC, 1))
    return dict(stretch_tokens=stretch_tokens, stretch_tail=stretch_tail, decode_tokens=decode_tokens, decode_tail=decode_tail, norm_gain=norm_gain, conv_taps=conv_taps, qkv_weight=qkv_weight, out_gain=out_gain, out_weight=out_weight, state_cache=state_cache, stretch_len=stretch_len, stretch_slot=stretch_slot, decode_slot=decode_slot, decode_owner=decode_owner)


def rms_rows(values, gain):
    values = values.astype(jnp.float32)
    factor = lax.rsqrt(lax.optimization_barrier(jnp.mean(values * values, axis=-1, keepdims=True)) + 1e-05)
    return values * factor * gain

def features(vectors):
    breadth = vectors.shape[-1]
    linear = vectors / math.sqrt(math.sqrt(breadth))
    outer = vectors[..., :, None] * vectors[..., None, :] / math.sqrt(2.0 * breadth)
    outer = outer.reshape(vectors.shape[:-1] + (breadth * breadth,))
    ones = jnp.ones(vectors.shape[:-1] + (1,), vectors.dtype)
    return jnp.concatenate([ones, linear, outer], axis=-1)

def convolve(tail, normed, conv_taps):
    joined = jnp.concatenate([tail, normed], axis=-2).astype(jnp.float32)
    span_rows = normed.shape[-2]
    total = conv_taps[0] * joined[..., 0:span_rows, :]
    total = total + conv_taps[1] * joined[..., 1:span_rows + 1, :]
    total = total + conv_taps[2] * joined[..., 2:span_rows + 2, :]
    return total.astype(jnp.bfloat16)

def project_out(attended, out_weight):
    row_total = attended.shape[0]
    share_width = H // N_HEAD * DH
    split_rows = attended.reshape(row_total, N_HEAD, share_width).astype(jnp.float32)
    grouped_weight = out_weight.reshape(N_HEAD, share_width, D).astype(jnp.float32)
    partial_value = jnp.einsum('ngk,gkd->gnd', split_rows, grouped_weight).astype(jnp.bfloat16)
    partial_value = lax.optimization_barrier(partial_value).astype(jnp.float32)
    return lax.optimization_barrier(jnp.sum(partial_value, axis=0)).astype(jnp.bfloat16)

def reference(stretch_tokens, stretch_tail, decode_tokens, decode_tail, norm_gain, conv_taps, qkv_weight, out_gain, out_weight, state_cache, stretch_len, stretch_slot, decode_slot, decode_owner):
    block_width = 2 * F + DH
    w_flat = qkv_weight.reshape(D, H * block_width)
    gains = out_gain.reshape(H, DH)

    def one_stretch(inputs):
        tokens, tail, length, slot_now, cache_group = inputs
        normed = rms_rows(tokens, norm_gain).astype(jnp.bfloat16)
        conved = convolve(tail, normed, conv_taps)
        qkv = jnp.dot(conved, w_flat, preferred_element_type=jnp.float32).astype(jnp.bfloat16)
        qkv = qkv.reshape(STRETCH, H, block_width).astype(jnp.float32)
        queries = qkv[:, :, :F]
        key_feats = qkv[:, :, F:2 * F]
        values = qkv[:, :, 2 * F:]
        positions = jnp.arange(STRETCH)
        valid_rows = positions < length
        state_old = lax.dynamic_index_in_dim(cache_group, slot_now.astype(jnp.int32), 0, keepdims=False)
        inner = jnp.einsum('ihf,jhf->hij', queries, key_feats) / math.sqrt(F)
        weights = 1.0 + inner + 0.5 * inner * inner
        allowed = (positions[None, :] <= positions[:, None]) & valid_rows[None, :]
        weights = jnp.where(allowed[None], weights, 0.0).astype(jnp.bfloat16)
        weights = lax.optimization_barrier(weights).astype(jnp.float32)
        local_sum = jnp.einsum('hij,jhd->ihd', weights, values)
        carried = jnp.einsum('ihp,hdp->ihd', features(queries), state_old, precision=lax.Precision.HIGHEST)
        attended = rms_rows(carried + local_sum, gains)
        attended = jnp.where(valid_rows[:, None, None], attended, 0.0).astype(jnp.bfloat16).reshape(STRETCH, H * DH)
        key_phi = jnp.where(valid_rows[:, None, None], features(key_feats), 0.0).astype(jnp.bfloat16)
        key_phi = lax.optimization_barrier(key_phi).astype(jnp.float32)
        state_next = state_old + jnp.einsum('jhd,jhp->hdp', values, key_phi, precision=lax.Precision.HIGHEST)
        return (project_out(attended, out_weight), state_next)
    stretch_out, state_new = lax.map(one_stretch, (stretch_tokens, stretch_tail, stretch_len, stretch_slot, state_cache))

    def one_decode(inputs):
        tokens, tail, owners, slots_now = inputs
        normed = rms_rows(tokens, norm_gain).astype(jnp.bfloat16)
        conved = convolve(tail, normed[:, None, :], conv_taps)[:, 0, :]
        qkv = jnp.dot(conved, w_flat, preferred_element_type=jnp.float32).astype(jnp.bfloat16)
        qkv = qkv.reshape(DEC, H, block_width).astype(jnp.float32)
        queries = qkv[:, :, :F]
        key_feats = qkv[:, :, F:2 * F]
        values = qkv[:, :, 2 * F:]
        states = state_cache[owners.astype(jnp.int32), slots_now.astype(jnp.int32)]
        carried = jnp.einsum('ehp,ehdp->ehd', features(queries), states, precision=lax.Precision.HIGHEST)
        inner = lax.optimization_barrier(jnp.sum(queries * key_feats, axis=-1)) / math.sqrt(F)
        own_term = (1.0 + inner + 0.5 * inner * inner)[..., None] * values
        attended = rms_rows(carried + own_term, gains).astype(jnp.bfloat16).reshape(DEC, H * DH)
        return project_out(attended, out_weight)
    decode_out = lax.map(one_decode, (decode_tokens, decode_tail, decode_owner[:, :, 0], decode_slot))
    return (stretch_out, decode_out, state_new)
```

```python
import math

import jax
import jax.numpy as jnp
from jax import lax
from jax.sharding import PartitionSpec as P

D = 1792
DH = 112
F = 16
STRETCH = 1024
DEC = 32


def from_behind(array, axis, by):
    peers = lax.axis_size(axis)
    pairs = [(i, i + by) for i in range(peers) if 0 <= i + by < peers]
    return lax.ppermute(array, axis, pairs)


def rms_rows(values, gain):
    values = values.astype(jnp.float32)
    factor = lax.rsqrt(jnp.mean(values * values, axis=-1, keepdims=True) + 1e-05)
    return values * factor * gain


def features(vectors):
    breadth = vectors.shape[-1]
    linear = vectors / math.sqrt(math.sqrt(breadth))
    outer = vectors[..., :, None] * vectors[..., None, :] / math.sqrt(2.0 * breadth)
    outer = outer.reshape(vectors.shape[:-1] + (breadth * breadth,))
    ones = jnp.ones(vectors.shape[:-1] + (1,), vectors.dtype)
    return jnp.concatenate([ones, linear, outer], axis=-1)


def convolve(tail, normed, conv_taps):
    joined = jnp.concatenate([tail, normed], axis=-2).astype(jnp.float32)
    span_rows = normed.shape[-2]
    total = conv_taps[0] * joined[..., 0:span_rows, :]
    total = total + conv_taps[1] * joined[..., 1 : span_rows + 1, :]
    total = total + conv_taps[2] * joined[..., 2 : span_rows + 2, :]
    return total.astype(jnp.bfloat16)


def decode_items(items, slot_items, cache_own, out_gain, head_count):
    item_count = items.shape[0]
    shaped = items.reshape(item_count, head_count, 2 * F + DH).astype(jnp.float32)
    queries = shaped[:, :, :F]
    key_feats = shaped[:, :, F : 2 * F]
    values = shaped[:, :, 2 * F :]
    slot_total = cache_own.shape[0]
    table = jnp.einsum(
        "nhp,shdp->nshd", features(queries), cache_own, precision=lax.Precision.HIGHEST
    )
    picker = (slot_items[:, None] == jnp.arange(slot_total)[None, :]).astype(jnp.float32)
    carried = jnp.einsum("ns,nshd->nhd", picker, table, precision=lax.Precision.HIGHEST)
    inner = jnp.sum(queries * key_feats, axis=-1) / math.sqrt(F)
    own_term = (1.0 + inner + 0.5 * inner * inner)[..., None] * values
    attended = rms_rows(carried + own_term, out_gain.reshape(head_count, DH))
    return attended.astype(jnp.bfloat16).reshape(item_count, head_count * DH)


def local(
    stretch_tokens,
    stretch_tail,
    decode_tokens,
    decode_tail,
    norm_gain,
    conv_taps,
    qkv_weight,
    out_gain,
    out_weight,
    state_cache,
    stretch_len,
    stretch_slot,
    decode_slot,
    decode_owner,
):
    head_count = qkv_weight.shape[1]
    block_width = qkv_weight.shape[2]
    rows_own = stretch_tokens.shape[1]
    w_flat = qkv_weight.reshape(D, head_count * block_width)
    gains = out_gain.reshape(head_count, DH)
    normed = rms_rows(stretch_tokens[0], norm_gain).astype(jnp.bfloat16)
    rim_rows = from_behind(normed[rows_own - 2 :], "head", 1)
    first_dev = lax.axis_index("head") == 0
    rim_rows = jnp.where(first_dev, stretch_tail[0], rim_rows)
    conved = convolve(rim_rows, normed, conv_taps)
    grouped = jnp.dot(
        lax.all_gather(conved, "head", axis=0, tiled=True),
        w_flat,
        preferred_element_type=jnp.float32,
    ).astype(jnp.bfloat16)
    grouped = grouped.reshape(STRETCH, head_count, block_width)
    queries = grouped[:, :, :F]
    key_feats = grouped[:, :, F : 2 * F]
    values = grouped[:, :, 2 * F :]
    length = stretch_len[0]
    positions = jnp.arange(STRETCH)
    valid_rows = positions < length
    state_old = lax.dynamic_index_in_dim(state_cache[0], stretch_slot[0], 0, keepdims=False)
    carried = jnp.einsum(
        "ihp,hdp->ihd",
        features(queries.astype(jnp.float32)),
        state_old,
        precision=lax.Precision.HIGHEST,
    )
    block_rows = min(512, STRETCH)
    pieces = []
    for anchor in range(0, STRETCH, block_rows):
        finish = anchor + block_rows
        inner = jnp.einsum(
            "ihf,jhf->hij",
            queries[anchor:finish],
            key_feats[:finish],
            preferred_element_type=jnp.float32,
        ) / math.sqrt(F)
        weights = 1.0 + inner + 0.5 * inner * inner
        allowed = (positions[None, :finish] <= positions[anchor:finish, None]) & valid_rows[
            None, :finish
        ]
        weights = jnp.where(allowed[None], weights, 0.0).astype(jnp.bfloat16)
        pieces.append(
            jnp.einsum("hij,jhd->ihd", weights, values[:finish], preferred_element_type=jnp.float32)
        )
    local_sum = jnp.concatenate(pieces, axis=0)
    attended = rms_rows(carried + local_sum, gains)
    attended = (
        jnp.where(valid_rows[:, None, None], attended, 0.0)
        .astype(jnp.bfloat16)
        .reshape(STRETCH, head_count * DH)
    )
    key_phi = jnp.where(
        valid_rows[:, None, None], features(key_feats.astype(jnp.float32)), 0.0
    ).astype(jnp.bfloat16)
    state_next = state_old + jnp.einsum(
        "jhd,jhp->hdp", values, key_phi, preferred_element_type=jnp.float32
    )
    stretch_part = jnp.dot(attended, out_weight, preferred_element_type=jnp.float32).astype(jnp.bfloat16)
    dec_normed = rms_rows(decode_tokens[0], norm_gain).astype(jnp.bfloat16)
    dec_conved = convolve(decode_tail[0], dec_normed[:, None, :], conv_taps)[:, 0, :]
    dec_qkv = jnp.dot(dec_conved, w_flat, preferred_element_type=jnp.float32).astype(jnp.bfloat16)
    owners = decode_owner[0, :, 0]
    slots_here = decode_slot[0]
    groups = lax.axis_size("tok")
    capacity = max(2, 2 * DEC // groups)
    earlier = jnp.arange(DEC)[None, :] < jnp.arange(DEC)[:, None]
    same_owner = owners[None, :] == owners[:, None]
    rank_in = jnp.sum(earlier & same_owner, axis=1)
    target = owners * capacity + rank_in
    placing = jnp.arange(groups * capacity)[:, None] == target[None, :]
    sent_rows = jnp.dot(
        placing.astype(jnp.bfloat16), dec_qkv, preferred_element_type=jnp.float32
    ).astype(jnp.bfloat16)
    sent_rows = sent_rows.reshape(groups, capacity, head_count * block_width)
    sent_slots = jnp.sum(jnp.where(placing, slots_here[None, :] + 1, 0), axis=1) - 1
    sent_slots = sent_slots.reshape(groups, capacity, 1).astype(jnp.bfloat16)
    sent_rows = jnp.concatenate([sent_rows, sent_slots], axis=2)
    item_rows = lax.all_to_all(sent_rows, "tok", split_axis=0, concat_axis=0, tiled=True)
    item_slots = item_rows[:, :, -1].astype(jnp.int32)
    item_rows = item_rows[:, :, :-1]
    item_count = item_rows.shape[1]
    flat_out = decode_items(
        item_rows.reshape(groups * item_count, head_count * block_width),
        item_slots.reshape(groups * item_count),
        state_cache[0],
        out_gain,
        head_count,
    )
    served = flat_out.reshape(groups, item_count, head_count * DH)
    returned = lax.all_to_all(served, "tok", split_axis=0, concat_axis=0, tiled=True)
    dec_attended = jnp.dot(
        jnp.transpose(placing).astype(jnp.bfloat16),
        returned.reshape(groups * capacity, head_count * DH),
        preferred_element_type=jnp.float32,
    ).astype(jnp.bfloat16)
    dec_part = jnp.dot(dec_attended, out_weight, preferred_element_type=jnp.float32).astype(jnp.bfloat16)
    heads = lax.axis_size("head")
    pad_rows = 16
    dec_part = dec_part.reshape(heads, DEC // heads, D)
    dec_part = jnp.pad(dec_part, ((0, 0), (0, pad_rows - DEC // heads), (0, 0)))
    both = jnp.concatenate([stretch_part.reshape(heads, rows_own, D), dec_part], axis=1)
    summed = lax.psum_scatter(
        both.reshape(heads * (rows_own + pad_rows), D), "head", scatter_dimension=0, tiled=True
    )
    stretch_out = summed[:rows_own]
    decode_out = summed[rows_own : rows_own + DEC // heads]
    return (stretch_out[None], decode_out[None], state_next[None])


def solution(mesh):
    in_specs = (
        P("tok", "head", None),
        P("tok", None, None),
        P("tok", None, None),
        P("tok", None, None, None),
        P(),
        P(),
        P(None, "head", None),
        P("head"),
        P("head", None),
        P("tok", None, "head", None, None),
        P("tok"),
        P("tok"),
        P("tok", None),
        P("tok", None, None),
    )
    out_specs = (P("tok", "head", None), P("tok", "head", None), P("tok", "head", None, None))
    return jax.shard_map(local, mesh=mesh, in_specs=in_specs, out_specs=out_specs, check_vma=False)
```

```python
import functools
import math

import jax
import jax.numpy as jnp
from jax import lax
from jax.experimental import pallas as pl
from jax.experimental.pallas import tpu as pltpu
from jax.sharding import PartitionSpec as P

D = 1792
DH = 112
F = 16
STRETCH = 1024
DEC = 32


SIDE = 4
MESH = pl.DeviceIdType.MESH


def plane_position():
    me = lax.axis_index("head")
    return me, lax.rem(me, SIDE), lax.div(me, SIDE)


def block_at(half, first, second, mx, my):
    dx, dy = (first, second) if half == 0 else (second, first)
    return lax.rem(my + dy % SIDE, SIDE) * SIDE + lax.rem(mx + dx % SIDE, SIDE)


def half_rows(half, quarter, rows):
    start = half * (rows // 2)
    if quarter is None:
        return pl.ds(start, rows // 2)
    return pl.ds(start + quarter * (rows // 4), rows // 4)


def greet(peers):
    barrier = pltpu.get_barrier_semaphore()
    for peer in peers:
        pl.semaphore_signal(barrier, inc=1, device_id={"head": peer}, device_id_type=MESH)
    pl.semaphore_wait(barrier, len(peers))


def gather_kernel(own_ref, w_ref, qkv_ref, buf, send_sem, recv_sem):
    me, mx, my = plane_position()
    rows = own_ref.shape[0]
    greet([block_at(0, d, 0, mx, my) for d in (1, -1)] + [block_at(0, 0, d, mx, my) for d in (1, -1)])
    sent = []

    def send(half, first, second, along_first, step, quarter=None):
        target = block_at(half, step if along_first else 0, 0 if along_first else step, mx, my)
        there = ((first - step) % SIDE, second) if along_first else (first, (second - step) % SIDE)
        block = block_at(half, first, second, mx, my)
        span = half_rows(half, quarter, rows)
        own = first == 0 and second == 0
        slot = half * 16 + there[0] * SIDE + there[1]
        copy = pltpu.make_async_remote_copy(
            src_ref=own_ref.at[span] if own else buf.at[block, span],
            dst_ref=buf.at[block, span],
            send_sem=send_sem.at[len(sent)],
            recv_sem=recv_sem.at[slot, quarter or 0],
            device_id={"head": target},
            device_id_type=MESH,
        )
        copy.start()
        sent.append(copy)

    def arrived(half, first, second, quarter=None):
        first, second = first % SIDE, second % SIDE
        place = buf.at[block_at(half, first, second, mx, my), half_rows(half, quarter, rows)]
        pltpu.make_async_remote_copy(
            src_ref=place,
            dst_ref=place,
            send_sem=send_sem.at[0],
            recv_sem=recv_sem.at[half * 16 + first * SIDE + second, quarter or 0],
            device_id={"head": block_at(0, 1, 0, mx, my)},
            device_id_type=MESH,
        ).wait_recv()

    def project(block, value):
        product = jnp.dot(value, w_ref[...], preferred_element_type=jnp.float32)
        qkv_ref[pl.ds(pl.multiple_of(block * rows, rows), rows), :] = product.astype(jnp.bfloat16)

    for along_first in (False, True):
        for half in (0, 1):
            for step in (1, -1):
                send(half, 0, 0, along_first, step)
    project(me, own_ref[...])
    for step in (1, -1):
        for half in (0, 1):
            origin = -step % SIDE
            arrived(half, origin, 0)
            send(half, origin, 0, True, step, 0 if step == 1 else 1)
            for out in (1, -1):
                send(half, origin, 0, False, out)

    def pass_on(half, first):
        for step in (1, -1):
            origin = -step % SIDE
            arrived(half, first, origin)
            send(half, first, origin, False, step, 0 if step == 1 else 1)

    for half in (0, 1):
        pass_on(half, 0)
    for half in (0, 1):
        for quarter in (0, 1):
            arrived(half, 2, 0, quarter)
        for out in (1, -1):
            send(half, 2, 0, False, out)
    for first in (3, 1, 2):
        for half in (0, 1):
            pass_on(half, first)
    for dx in (1, 3, 0):
        for dy in (1, 3, 0):
            if dx or dy:
                block = block_at(0, dx, dy, mx, my)
                project(block, buf[block])
    for first in (0, 3, 1, 2):
        for half in (0, 1):
            for quarter in (0, 1):
                arrived(half, first, 2, quarter)
        for dx, dy in {(first, 2), (2, first)}:
            block = block_at(0, dx, dy, mx, my)
            project(block, buf[block])
    for copy in sent:
        copy.wait_send()


def gather_project(conved, weight):
    rows, width = conved.shape
    columns = weight.shape[1]
    whole = pl.BlockSpec(memory_space=pltpu.VMEM)
    return pl.pallas_call(
        gather_kernel,
        out_shape=jax.ShapeDtypeStruct((16 * rows, columns), jnp.bfloat16),
        in_specs=[whole, whole],
        out_specs=whole,
        scratch_shapes=[
            pltpu.VMEM((16, rows, width), jnp.bfloat16),
            pltpu.SemaphoreType.DMA((40,)),
            pltpu.SemaphoreType.DMA((32, 2)),
        ],
        compiler_params=pltpu.CompilerParams(
            collective_id=0, has_side_effects=True, vmem_limit_bytes=40 * 2**20
        ),
        name="gather_project",
    )(conved, weight)


def scatter_kernel(
    rows, att_ref, w_ref, dec_ref, out_ref, dec_out_ref,
    part, far, near, far_last, near_last, dec_in, send_sem, far_sem, near_sem, dec_send, dec_recv,
):
    me, mx, my = plane_position()
    peers = [lax.rem(me + k, 16) for k in range(1, 16)]
    greet(peers)
    dec_copies = []
    for k, peer in enumerate(peers):
        copy = pltpu.make_async_remote_copy(
            src_ref=dec_ref.at[peer],
            dst_ref=dec_in.at[k],
            send_sem=dec_send.at[k],
            recv_sem=dec_recv.at[k],
            device_id={"head": peer},
            device_id_type=MESH,
        )
        copy.start()
        dec_copies.append(copy)
    sent = []

    def send(half, along_first, step, source, target_ref, sem):
        copy = pltpu.make_async_remote_copy(
            src_ref=source,
            dst_ref=target_ref,
            send_sem=send_sem.at[len(sent)],
            recv_sem=sem,
            device_id={
                "head": block_at(half, step if along_first else 0, 0 if along_first else step, mx, my)
            },
            device_id_type=MESH,
        )
        copy.start()
        sent.append(copy)

    def arrived(place, sem):
        pltpu.make_async_remote_copy(
            src_ref=place,
            dst_ref=place,
            send_sem=send_sem.at[0],
            recv_sem=sem,
            device_id={"head": block_at(0, 1, 0, mx, my)},
            device_id_type=MESH,
        ).wait_recv()

    def project(dx, dy):
        block = block_at(0, dx, dy, mx, my)
        value = att_ref[pl.ds(pl.multiple_of(block * rows, rows), rows), :]
        product = jnp.dot(value, w_ref[...], preferred_element_type=jnp.float32)
        part[block] = product.astype(jnp.bfloat16)

    def piece(half, first, second, quarter=None):
        return block_at(half, first, second, mx, my), half_rows(half, quarter, rows)

    def wide(value):
        return value.astype(jnp.float32)

    def send_far(half, first):
        for quarter, step in ((0, -1), (1, 1)):
            block, span = piece(half, first, 2, quarter)
            slot = half * SIDE + first
            send(half, False, step, part.at[block, span], far.at[slot, quarter], far_sem.at[slot, quarter])

    order = (2, 1, 3, 0)
    for first in order:
        for dx, dy in sorted({(first, 2), (2, first)}):
            project(dx, dy)
        for half in (0, 1):
            send_far(half, first)
    for dx in (1, 3, 0):
        for dy in (1, 3, 0):
            project(dx, dy)
    for first in order:
        for half in (0, 1):
            slot = half * SIDE + first
            for quarter, step in ((0, -1), (1, 1)):
                arrived(far.at[slot, quarter], far_sem.at[slot, quarter])
                block, span = piece(half, first, step, quarter)
                part[block, span, :] = (wide(part[block, span, :]) + wide(far[slot, quarter])).astype(jnp.bfloat16)
                block, span = piece(half, first, step)
                send(half, False, step, part.at[block, span], near.at[slot, quarter], near_sem.at[slot, quarter])
    for first in order:
        for half in (0, 1):
            slot = half * SIDE + first
            for quarter in (0, 1):
                arrived(near.at[slot, quarter], near_sem.at[slot, quarter])
            block, span = piece(half, first, 0)
            if first == 0:
                continue
            total = wide(part[block, span, :]) + wide(near[slot, 0]) + wide(near[slot, 1])
            part[block, span, :] = total.astype(jnp.bfloat16)
            if first == 2:
                for quarter, step in ((0, -1), (1, 1)):
                    block, span = piece(half, 2, 0, quarter)
                    send(half, True, step, part.at[block, span], far_last.at[half, quarter], far_sem.at[8 + half, quarter])
            else:
                quarter, step = (1, 1) if first == 1 else (0, -1)
                arrived(far_last.at[half, quarter], far_sem.at[8 + half, quarter])
                inner, inner_span = piece(half, step, 0, quarter)
                part[inner, inner_span, :] = (
                    wide(part[inner, inner_span, :]) + wide(far_last[half, quarter])
                ).astype(jnp.bfloat16)
                send(half, True, step, part.at[block, span], near_last.at[half, quarter], near_sem.at[8 + half, quarter])
    dec_total = wide(dec_ref[me])
    for k, copy in enumerate(dec_copies):
        copy.wait_recv()
        dec_total = dec_total + wide(dec_in[k])
    dec_out_ref[...] = dec_total.astype(jnp.bfloat16)
    for half in (0, 1):
        block, span = piece(half, 0, 0)
        total = wide(part[block, span, :]) + wide(near[half * SIDE, 0]) + wide(near[half * SIDE, 1])
        for quarter in (0, 1):
            arrived(near_last.at[half, quarter], near_sem.at[8 + half, quarter])
            total = total + wide(near_last[half, quarter])
        out_ref[span, :] = total.astype(jnp.bfloat16)
    for copy in sent:
        copy.wait_send()
    for copy in dec_copies:
        copy.wait_send()


def project_scatter(attended, weight, dec_parts):
    rows = attended.shape[0] // 16
    width = weight.shape[1]
    whole = pl.BlockSpec(memory_space=pltpu.VMEM)
    return pl.pallas_call(
        functools.partial(scatter_kernel, rows),
        out_shape=(
            jax.ShapeDtypeStruct((rows, width), jnp.bfloat16),
            jax.ShapeDtypeStruct(dec_parts.shape[1:], jnp.bfloat16),
        ),
        in_specs=[whole, whole, whole],
        out_specs=(whole, whole),
        scratch_shapes=[
            pltpu.VMEM((16, rows, width), jnp.bfloat16),
            pltpu.VMEM((8, 2, rows // 4, width), jnp.bfloat16),
            pltpu.VMEM((8, 2, rows // 2, width), jnp.bfloat16),
            pltpu.VMEM((2, 2, rows // 4, width), jnp.bfloat16),
            pltpu.VMEM((2, 2, rows // 2, width), jnp.bfloat16),
            pltpu.VMEM((15,) + dec_parts.shape[1:], jnp.bfloat16),
            pltpu.SemaphoreType.DMA((40,)),
            pltpu.SemaphoreType.DMA((10, 2)),
            pltpu.SemaphoreType.DMA((10, 2)),
            pltpu.SemaphoreType.DMA((15,)),
            pltpu.SemaphoreType.DMA((15,)),
        ],
        compiler_params=pltpu.CompilerParams(
            collective_id=1, has_side_effects=True, vmem_limit_bytes=40 * 2**20
        ),
        name="project_scatter",
    )(attended, weight, dec_parts)


def from_behind(array, axis, by):
    peers = lax.axis_size(axis)
    pairs = [(i, i + by) for i in range(peers) if 0 <= i + by < peers]
    return lax.ppermute(array, axis, pairs)


def rms_rows(values, gain):
    values = values.astype(jnp.float32)
    factor = lax.rsqrt(jnp.mean(values * values, axis=-1, keepdims=True) + 1e-05)
    return values * factor * gain


def features(vectors):
    breadth = vectors.shape[-1]
    linear = vectors / math.sqrt(math.sqrt(breadth))
    outer = vectors[..., :, None] * vectors[..., None, :] / math.sqrt(2.0 * breadth)
    outer = outer.reshape(vectors.shape[:-1] + (breadth * breadth,))
    ones = jnp.ones(vectors.shape[:-1] + (1,), vectors.dtype)
    return jnp.concatenate([ones, linear, outer], axis=-1)


def convolve(tail, normed, conv_taps):
    joined = jnp.concatenate([tail, normed], axis=-2).astype(jnp.float32)
    span_rows = normed.shape[-2]
    total = conv_taps[0] * joined[..., 0:span_rows, :]
    total = total + conv_taps[1] * joined[..., 1 : span_rows + 1, :]
    total = total + conv_taps[2] * joined[..., 2 : span_rows + 2, :]
    return total.astype(jnp.bfloat16)


def decode_items(items, slot_items, cache_own, out_gain, head_count):
    item_count = items.shape[0]
    shaped = items.reshape(item_count, head_count, 2 * F + DH).astype(jnp.float32)
    queries = shaped[:, :, :F]
    key_feats = shaped[:, :, F : 2 * F]
    values = shaped[:, :, 2 * F :]
    slot_total = cache_own.shape[0]
    table = jnp.einsum(
        "nhp,shdp->nshd", features(queries), cache_own, precision=lax.Precision.HIGHEST
    )
    picker = (slot_items[:, None] == jnp.arange(slot_total)[None, :]).astype(jnp.float32)
    carried = jnp.einsum("ns,nshd->nhd", picker, table, precision=lax.Precision.HIGHEST)
    inner = jnp.sum(queries * key_feats, axis=-1) / math.sqrt(F)
    own_term = (1.0 + inner + 0.5 * inner * inner)[..., None] * values
    attended = rms_rows(carried + own_term, out_gain.reshape(head_count, DH))
    return attended.astype(jnp.bfloat16).reshape(item_count, head_count * DH)


def local(
    stretch_tokens,
    stretch_tail,
    decode_tokens,
    decode_tail,
    norm_gain,
    conv_taps,
    qkv_weight,
    out_gain,
    out_weight,
    state_cache,
    stretch_len,
    stretch_slot,
    decode_slot,
    decode_owner,
):
    head_count = qkv_weight.shape[1]
    block_width = qkv_weight.shape[2]
    rows_own = stretch_tokens.shape[1]
    w_flat = qkv_weight.reshape(D, head_count * block_width)
    gains = out_gain.reshape(head_count, DH)
    normed = rms_rows(stretch_tokens[0], norm_gain).astype(jnp.bfloat16)
    rim_rows = from_behind(normed[rows_own - 2 :], "head", 1)
    first_dev = lax.axis_index("head") == 0
    rim_rows = jnp.where(first_dev, stretch_tail[0], rim_rows)
    conved = convolve(rim_rows, normed, conv_taps)
    grouped = gather_project(conved, w_flat)
    grouped = grouped.reshape(STRETCH, head_count, block_width)
    queries = grouped[:, :, :F]
    key_feats = grouped[:, :, F : 2 * F]
    values = grouped[:, :, 2 * F :]
    length = stretch_len[0]
    positions = jnp.arange(STRETCH)
    valid_rows = positions < length
    state_old = lax.dynamic_index_in_dim(state_cache[0], stretch_slot[0], 0, keepdims=False)
    carried = jnp.einsum(
        "ihp,hdp->ihd",
        features(queries.astype(jnp.float32)),
        state_old,
        precision=lax.Precision.HIGHEST,
    )
    block_rows = min(512, STRETCH)
    pieces = []
    for anchor in range(0, STRETCH, block_rows):
        finish = anchor + block_rows
        inner = jnp.einsum(
            "ihf,jhf->hij",
            queries[anchor:finish],
            key_feats[:finish],
            preferred_element_type=jnp.float32,
        ) / math.sqrt(F)
        weights = 1.0 + inner + 0.5 * inner * inner
        allowed = (positions[None, :finish] <= positions[anchor:finish, None]) & valid_rows[
            None, :finish
        ]
        weights = jnp.where(allowed[None], weights, 0.0).astype(jnp.bfloat16)
        pieces.append(
            jnp.einsum("hij,jhd->ihd", weights, values[:finish], preferred_element_type=jnp.float32)
        )
    local_sum = jnp.concatenate(pieces, axis=0)
    attended = rms_rows(carried + local_sum, gains)
    attended = (
        jnp.where(valid_rows[:, None, None], attended, 0.0)
        .astype(jnp.bfloat16)
        .reshape(STRETCH, head_count * DH)
    )
    key_phi = jnp.where(
        valid_rows[:, None, None], features(key_feats.astype(jnp.float32)), 0.0
    ).astype(jnp.bfloat16)
    state_next = state_old + jnp.einsum(
        "jhd,jhp->hdp", values, key_phi, preferred_element_type=jnp.float32
    )
    dec_normed = rms_rows(decode_tokens[0], norm_gain).astype(jnp.bfloat16)
    dec_conved = convolve(decode_tail[0], dec_normed[:, None, :], conv_taps)[:, 0, :]
    dec_qkv = jnp.dot(dec_conved, w_flat, preferred_element_type=jnp.float32).astype(jnp.bfloat16)
    owners = decode_owner[0, :, 0]
    slots_here = decode_slot[0]
    groups = lax.axis_size("tok")
    capacity = max(2, 2 * DEC // groups)
    earlier = jnp.arange(DEC)[None, :] < jnp.arange(DEC)[:, None]
    same_owner = owners[None, :] == owners[:, None]
    rank_in = jnp.sum(earlier & same_owner, axis=1)
    target = owners * capacity + rank_in
    placing = jnp.arange(groups * capacity)[:, None] == target[None, :]
    sent_rows = jnp.dot(
        placing.astype(jnp.bfloat16), dec_qkv, preferred_element_type=jnp.float32
    ).astype(jnp.bfloat16)
    sent_rows = sent_rows.reshape(groups, capacity, head_count * block_width)
    sent_slots = jnp.sum(jnp.where(placing, slots_here[None, :] + 1, 0), axis=1) - 1
    sent_slots = sent_slots.reshape(groups, capacity, 1).astype(jnp.bfloat16)
    sent_rows = jnp.concatenate([sent_rows, sent_slots], axis=2)
    item_rows = lax.all_to_all(sent_rows, "tok", split_axis=0, concat_axis=0, tiled=True)
    item_slots = item_rows[:, :, -1].astype(jnp.int32)
    item_rows = item_rows[:, :, :-1]
    item_count = item_rows.shape[1]
    flat_out = decode_items(
        item_rows.reshape(groups * item_count, head_count * block_width),
        item_slots.reshape(groups * item_count),
        state_cache[0],
        out_gain,
        head_count,
    )
    served = flat_out.reshape(groups, item_count, head_count * DH)
    returned = lax.all_to_all(served, "tok", split_axis=0, concat_axis=0, tiled=True)
    dec_attended = jnp.dot(
        jnp.transpose(placing).astype(jnp.bfloat16),
        returned.reshape(groups * capacity, head_count * DH),
        preferred_element_type=jnp.float32,
    ).astype(jnp.bfloat16)
    dec_part = jnp.dot(dec_attended, out_weight, preferred_element_type=jnp.float32).astype(jnp.bfloat16)
    heads = lax.axis_size("head")
    lanes = 128
    dec_part = dec_part.reshape(heads, DEC // heads * D // lanes, lanes)
    used = dec_part.shape[1]
    dec_part = jnp.pad(dec_part, ((0, 0), (0, -used % 16), (0, 0)))
    stretch_out, dec_sum = project_scatter(attended, out_weight, dec_part)
    decode_out = dec_sum[:used].reshape(DEC // heads, D)
    return (stretch_out[None], decode_out[None], state_next[None])


def solution(mesh):
    in_specs = (
        P("tok", "head", None),
        P("tok", None, None),
        P("tok", None, None),
        P("tok", None, None, None),
        P(),
        P(),
        P(None, "head", None),
        P("head"),
        P("head", None),
        P("tok", None, "head", None, None),
        P("tok"),
        P("tok"),
        P("tok", None),
        P("tok", None, None),
    )
    out_specs = (P("tok", "head", None), P("tok", "head", None), P("tok", "head", None, None))
    return jax.shard_map(local, mesh=mesh, in_specs=in_specs, out_specs=out_specs, check_vma=False)
```

```python
import functools
import math

import jax
import jax.numpy as jnp
from jax import lax
from jax.experimental import pallas as pl
from jax.experimental.pallas import tpu as pltpu
from jax.sharding import PartitionSpec as P

D = 1792
DH = 112
F = 16
STRETCH = 1024
DEC = 32


SIDE = 4
MESH = pl.DeviceIdType.MESH


def plane_position():
    me = lax.axis_index("head")
    return me, lax.rem(me, SIDE), lax.div(me, SIDE)


def block_at(half, first, second, mx, my):
    dx, dy = (first, second) if half == 0 else (second, first)
    return lax.rem(my + dy % SIDE, SIDE) * SIDE + lax.rem(mx + dx % SIDE, SIDE)


def half_rows(half, quarter, rows):
    start = half * (rows // 2)
    if quarter is None:
        return pl.ds(start, rows // 2)
    return pl.ds(start + quarter * (rows // 4), rows // 4)


def greet(peers):
    barrier = pltpu.get_barrier_semaphore()
    for peer in peers:
        pl.semaphore_signal(barrier, inc=1, device_id={"head": peer}, device_id_type=MESH)
    groups, mine = lax.axis_size("tok"), lax.axis_index("tok")

    def hail(k, carry):
        pl.semaphore_signal(
            barrier, inc=1, device_id={"tok": lax.rem(mine + k, groups)}, device_id_type=MESH
        )
        return carry

    lax.fori_loop(1, groups, hail, 0)
    return barrier, len(peers) + groups - 1


def swap_copy(k, source, landing, send_sem, recv_sem):
    groups, mine = lax.axis_size("tok"), lax.axis_index("tok")
    peer = lax.rem(mine + k, groups)
    return pltpu.make_async_remote_copy(
        src_ref=source.at[peer],
        dst_ref=landing.at[mine],
        send_sem=send_sem.at[k],
        recv_sem=recv_sem.at[k],
        device_id={"tok": peer},
        device_id_type=MESH,
    )


def swap_start(source, landing, send_sem, recv_sem):
    def body(k, carry):
        swap_copy(k, source, landing, send_sem, recv_sem).start()
        return carry

    lax.fori_loop(1, lax.axis_size("tok"), body, 0)


def swap_finish(source, landing, send_sem, recv_sem):
    groups, mine = lax.axis_size("tok"), lax.axis_index("tok")

    def body(k, carry):
        origin = lax.rem(mine + groups - k, groups)
        pltpu.make_async_remote_copy(
            src_ref=landing.at[origin],
            dst_ref=landing.at[origin],
            send_sem=send_sem.at[k],
            recv_sem=recv_sem.at[k],
            device_id={"tok": lax.rem(mine + k, groups)},
            device_id_type=MESH,
        ).wait_recv()
        swap_copy(k, source, landing, send_sem, recv_sem).wait_send()
        return carry

    lax.fori_loop(1, groups, body, 0)
    landing[mine] = source[mine]


def gather_kernel(
    own_ref, w_ref, items_ref, qkv_ref, got_ref, buf, landing, send_sem, recv_sem, swap_send, swap_recv
):
    me, mx, my = plane_position()
    rows = own_ref.shape[0]
    barrier, callers = greet(
        [block_at(0, d, 0, mx, my) for d in (1, -1)] + [block_at(0, 0, d, mx, my) for d in (1, -1)]
    )
    sent = []

    def send(half, first, second, along_first, step, quarter=None):
        target = block_at(half, step if along_first else 0, 0 if along_first else step, mx, my)
        there = ((first - step) % SIDE, second) if along_first else (first, (second - step) % SIDE)
        block = block_at(half, first, second, mx, my)
        span = half_rows(half, quarter, rows)
        own = first == 0 and second == 0
        slot = half * 16 + there[0] * SIDE + there[1]
        copy = pltpu.make_async_remote_copy(
            src_ref=own_ref.at[span] if own else buf.at[block, span],
            dst_ref=buf.at[block, span],
            send_sem=send_sem.at[len(sent)],
            recv_sem=recv_sem.at[slot, quarter or 0],
            device_id={"head": target},
            device_id_type=MESH,
        )
        copy.start()
        sent.append(copy)

    def arrived(half, first, second, quarter=None):
        first, second = first % SIDE, second % SIDE
        place = buf.at[block_at(half, first, second, mx, my), half_rows(half, quarter, rows)]
        pltpu.make_async_remote_copy(
            src_ref=place,
            dst_ref=place,
            send_sem=send_sem.at[0],
            recv_sem=recv_sem.at[half * 16 + first * SIDE + second, quarter or 0],
            device_id={"head": block_at(0, 1, 0, mx, my)},
            device_id_type=MESH,
        ).wait_recv()

    def project(block, value):
        product = jnp.dot(value, w_ref[...], preferred_element_type=jnp.float32)
        qkv_ref[pl.ds(pl.multiple_of(block * rows, rows), rows), :] = product.astype(jnp.bfloat16)

    project(me, own_ref[...])
    pl.semaphore_wait(barrier, callers)
    for along_first in (False, True):
        for half in (0, 1):
            for step in (1, -1):
                send(half, 0, 0, along_first, step)
    swap_start(items_ref, landing, swap_send, swap_recv)
    for step in (1, -1):
        for half in (0, 1):
            origin = -step % SIDE
            arrived(half, origin, 0)
            send(half, origin, 0, True, step, 0 if step == 1 else 1)
            for out in (1, -1):
                send(half, origin, 0, False, out)

    def pass_on(half, first):
        for step in (1, -1):
            origin = -step % SIDE
            arrived(half, first, origin)
            send(half, first, origin, False, step, 0 if step == 1 else 1)

    for half in (0, 1):
        pass_on(half, 0)
    for half in (0, 1):
        for quarter in (0, 1):
            arrived(half, 2, 0, quarter)
        for out in (1, -1):
            send(half, 2, 0, False, out)
    for first in (3, 1, 2):
        for half in (0, 1):
            pass_on(half, first)
    swap_finish(items_ref, landing, swap_send, swap_recv)
    got_ref[...] = landing[...]
    for dx in (1, 3, 0):
        for dy in (1, 3, 0):
            if dx or dy:
                block = block_at(0, dx, dy, mx, my)
                project(block, buf[block])
    for first in (0, 3, 1, 2):
        for half in (0, 1):
            for quarter in (0, 1):
                arrived(half, first, 2, quarter)
        for dx, dy in {(first, 2), (2, first)}:
            block = block_at(0, dx, dy, mx, my)
            project(block, buf[block])
    for copy in sent:
        copy.wait_send()


def gather_project(conved, weight, items):
    rows, width = conved.shape
    columns = weight.shape[1]
    whole = pl.BlockSpec(memory_space=pltpu.VMEM)
    return pl.pallas_call(
        gather_kernel,
        out_shape=(
            jax.ShapeDtypeStruct((16 * rows, columns), jnp.bfloat16),
            jax.ShapeDtypeStruct(items.shape, items.dtype),
        ),
        in_specs=[whole, whole, whole],
        out_specs=(whole, whole),
        scratch_shapes=[
            pltpu.VMEM((16, rows, width), jnp.bfloat16),
            pltpu.VMEM(items.shape, items.dtype),
            pltpu.SemaphoreType.DMA((40,)),
            pltpu.SemaphoreType.DMA((32, 2)),
            pltpu.SemaphoreType.DMA((items.shape[0],)),
            pltpu.SemaphoreType.DMA((items.shape[0],)),
        ],
        compiler_params=pltpu.CompilerParams(
            collective_id=0, has_side_effects=True, vmem_limit_bytes=40 * 2**20
        ),
        name="gather_project",
    )(conved, weight, items)


def scatter_kernel(
    rows, att_ref, w_ref, served_ref, place_ref, out_ref, dec_out_ref,
    part, far, near, far_last, near_last, landing, dec_wide, dec_ref, dec_in,
    send_sem, far_sem, near_sem, dec_send, dec_recv, swap_send, swap_recv,
):
    me, mx, my = plane_position()
    peers = [lax.rem(me + k, 16) for k in range(1, 16)]
    barrier, callers = greet(peers)
    sent = []

    def send(half, along_first, step, source, target_ref, sem):
        copy = pltpu.make_async_remote_copy(
            src_ref=source,
            dst_ref=target_ref,
            send_sem=send_sem.at[len(sent)],
            recv_sem=sem,
            device_id={
                "head": block_at(half, step if along_first else 0, 0 if along_first else step, mx, my)
            },
            device_id_type=MESH,
        )
        copy.start()
        sent.append(copy)

    def arrived(place, sem):
        pltpu.make_async_remote_copy(
            src_ref=place,
            dst_ref=place,
            send_sem=send_sem.at[0],
            recv_sem=sem,
            device_id={"head": block_at(0, 1, 0, mx, my)},
            device_id_type=MESH,
        ).wait_recv()

    def project(dx, dy):
        block = block_at(0, dx, dy, mx, my)
        value = att_ref[pl.ds(pl.multiple_of(block * rows, rows), rows), :]
        product = jnp.dot(value, w_ref[...], preferred_element_type=jnp.float32)
        part[block] = product.astype(jnp.bfloat16)

    def piece(half, first, second, quarter=None):
        return block_at(half, first, second, mx, my), half_rows(half, quarter, rows)

    def wide(value):
        return value.astype(jnp.float32)

    def send_far(half, first):
        for quarter, step in ((0, -1), (1, 1)):
            block, span = piece(half, first, 2, quarter)
            slot = half * SIDE + first
            send(half, False, step, part.at[block, span], far.at[slot, quarter], far_sem.at[slot, quarter])

    order = (2, 1, 3, 0)
    for first in order:
        for dx, dy in sorted({(first, 2), (2, first)}):
            project(dx, dy)
    for dx, dy in ((1, 1), (1, 3), (3, 1), (3, 3), (0, 1), (1, 0)):
        project(dx, dy)
    pl.semaphore_wait(barrier, callers)
    for first in order:
        for half in (0, 1):
            send_far(half, first)
    swap_start(served_ref, landing, swap_send, swap_recv)
    for dx, dy in ((3, 0), (0, 3), (0, 0)):
        project(dx, dy)
    for first in order:
        for half in (0, 1):
            slot = half * SIDE + first
            for quarter, step in ((0, -1), (1, 1)):
                arrived(far.at[slot, quarter], far_sem.at[slot, quarter])
                block, span = piece(half, first, step, quarter)
                part[block, span, :] = (wide(part[block, span, :]) + wide(far[slot, quarter])).astype(jnp.bfloat16)
                block, span = piece(half, first, step)
                send(half, False, step, part.at[block, span], near.at[slot, quarter], near_sem.at[slot, quarter])
    swap_finish(served_ref, landing, swap_send, swap_recv)
    groups, item_rows, lanes = landing.shape
    returned = landing[...].reshape(groups * item_rows, lanes).astype(jnp.bfloat16)
    dec_att = jnp.dot(place_ref[...], returned, preferred_element_type=jnp.float32)
    dec_att = dec_att.astype(jnp.bfloat16)[:, : w_ref.shape[0]]
    dec_part = jnp.dot(dec_att, w_ref[...], preferred_element_type=jnp.float32)
    dec_wide[...] = jnp.zeros(dec_wide.shape, jnp.float32)
    per_peer = dec_part.shape[0] // 16
    for chunk in range(dec_part.shape[1] // lanes):
        for row in range(per_peer):
            dec_wide[:, chunk * per_peer + row, :] = dec_part[
                row * 16 : row * 16 + 16, chunk * lanes : (chunk + 1) * lanes
            ]
    dec_ref[...] = dec_wide[...].astype(jnp.bfloat16)
    dec_copies = []
    for k, peer in enumerate(peers):
        copy = pltpu.make_async_remote_copy(
            src_ref=dec_ref.at[peer],
            dst_ref=dec_in.at[k],
            send_sem=dec_send.at[k],
            recv_sem=dec_recv.at[k],
            device_id={"head": peer},
            device_id_type=MESH,
        )
        copy.start()
        dec_copies.append(copy)
    for first in order:
        for half in (0, 1):
            slot = half * SIDE + first
            for quarter in (0, 1):
                arrived(near.at[slot, quarter], near_sem.at[slot, quarter])
            block, span = piece(half, first, 0)
            if first == 0:
                continue
            total = wide(part[block, span, :]) + wide(near[slot, 0]) + wide(near[slot, 1])
            part[block, span, :] = total.astype(jnp.bfloat16)
            if first == 2:
                for quarter, step in ((0, -1), (1, 1)):
                    block, span = piece(half, 2, 0, quarter)
                    send(half, True, step, part.at[block, span], far_last.at[half, quarter], far_sem.at[8 + half, quarter])
            else:
                quarter, step = (1, 1) if first == 1 else (0, -1)
                arrived(far_last.at[half, quarter], far_sem.at[8 + half, quarter])
                inner, inner_span = piece(half, step, 0, quarter)
                part[inner, inner_span, :] = (
                    wide(part[inner, inner_span, :]) + wide(far_last[half, quarter])
                ).astype(jnp.bfloat16)
                send(half, True, step, part.at[block, span], near_last.at[half, quarter], near_sem.at[8 + half, quarter])
    dec_total = wide(dec_ref[me])
    for k, copy in enumerate(dec_copies):
        copy.wait_recv()
        dec_total = dec_total + wide(dec_in[k])
    dec_out_ref[...] = dec_total.astype(jnp.bfloat16)
    for half in (0, 1):
        block, span = piece(half, 0, 0)
        total = wide(part[block, span, :]) + wide(near[half * SIDE, 0]) + wide(near[half * SIDE, 1])
        for quarter in (0, 1):
            arrived(near_last.at[half, quarter], near_sem.at[8 + half, quarter])
            total = total + wide(near_last[half, quarter])
        out_ref[span, :] = total.astype(jnp.bfloat16)
    for copy in sent:
        copy.wait_send()
    for copy in dec_copies:
        copy.wait_send()


def project_scatter(attended, weight, served, placing):
    rows = attended.shape[0] // 16
    width = weight.shape[1]
    lanes = served.shape[2]
    dec_rows = -(-placing.shape[0] // 16 * width // lanes // 16) * 16
    whole = pl.BlockSpec(memory_space=pltpu.VMEM)
    return pl.pallas_call(
        functools.partial(scatter_kernel, rows),
        out_shape=(
            jax.ShapeDtypeStruct((rows, width), jnp.bfloat16),
            jax.ShapeDtypeStruct((dec_rows, lanes), jnp.bfloat16),
        ),
        in_specs=[whole, whole, whole, whole],
        out_specs=(whole, whole),
        scratch_shapes=[
            pltpu.VMEM((16, rows, width), jnp.bfloat16),
            pltpu.VMEM((8, 2, rows // 4, width), jnp.bfloat16),
            pltpu.VMEM((8, 2, rows // 2, width), jnp.bfloat16),
            pltpu.VMEM((2, 2, rows // 4, width), jnp.bfloat16),
            pltpu.VMEM((2, 2, rows // 2, width), jnp.bfloat16),
            pltpu.VMEM(served.shape, served.dtype),
            pltpu.VMEM((16, dec_rows, lanes), jnp.float32),
            pltpu.VMEM((16, dec_rows, lanes), jnp.bfloat16),
            pltpu.VMEM((15, dec_rows, lanes), jnp.bfloat16),
            pltpu.SemaphoreType.DMA((40,)),
            pltpu.SemaphoreType.DMA((10, 2)),
            pltpu.SemaphoreType.DMA((10, 2)),
            pltpu.SemaphoreType.DMA((15,)),
            pltpu.SemaphoreType.DMA((15,)),
            pltpu.SemaphoreType.DMA((served.shape[0],)),
            pltpu.SemaphoreType.DMA((served.shape[0],)),
        ],
        compiler_params=pltpu.CompilerParams(
            collective_id=1, has_side_effects=True, vmem_limit_bytes=40 * 2**20
        ),
        name="project_scatter",
    )(attended, weight, served, placing)


def from_behind(array, axis, by):
    peers = lax.axis_size(axis)
    pairs = [(i, i + by) for i in range(peers) if 0 <= i + by < peers]
    return lax.ppermute(array, axis, pairs)


def rms_rows(values, gain):
    values = values.astype(jnp.float32)
    factor = lax.rsqrt(jnp.mean(values * values, axis=-1, keepdims=True) + 1e-05)
    return values * factor * gain


def features(vectors):
    breadth = vectors.shape[-1]
    linear = vectors / math.sqrt(math.sqrt(breadth))
    outer = vectors[..., :, None] * vectors[..., None, :] / math.sqrt(2.0 * breadth)
    outer = outer.reshape(vectors.shape[:-1] + (breadth * breadth,))
    ones = jnp.ones(vectors.shape[:-1] + (1,), vectors.dtype)
    return jnp.concatenate([ones, linear, outer], axis=-1)


def convolve(tail, normed, conv_taps):
    joined = jnp.concatenate([tail, normed], axis=-2).astype(jnp.float32)
    span_rows = normed.shape[-2]
    total = conv_taps[0] * joined[..., 0:span_rows, :]
    total = total + conv_taps[1] * joined[..., 1 : span_rows + 1, :]
    total = total + conv_taps[2] * joined[..., 2 : span_rows + 2, :]
    return total.astype(jnp.bfloat16)


def decode_items(items, slot_items, cache_own, out_gain, head_count):
    item_count = items.shape[0]
    shaped = items.reshape(item_count, head_count, 2 * F + DH).astype(jnp.float32)
    queries = shaped[:, :, :F]
    key_feats = shaped[:, :, F : 2 * F]
    values = shaped[:, :, 2 * F :]
    slot_total = cache_own.shape[0]
    table = jnp.einsum(
        "nhp,shdp->nshd", features(queries), cache_own, precision=lax.Precision.HIGHEST
    )
    picker = (slot_items[:, None] == jnp.arange(slot_total)[None, :]).astype(jnp.float32)
    carried = jnp.einsum("ns,nshd->nhd", picker, table, precision=lax.Precision.HIGHEST)
    inner = jnp.sum(queries * key_feats, axis=-1) / math.sqrt(F)
    own_term = (1.0 + inner + 0.5 * inner * inner)[..., None] * values
    attended = rms_rows(carried + own_term, out_gain.reshape(head_count, DH))
    return attended.astype(jnp.bfloat16).reshape(item_count, head_count * DH)


def local(
    stretch_tokens,
    stretch_tail,
    decode_tokens,
    decode_tail,
    norm_gain,
    conv_taps,
    qkv_weight,
    out_gain,
    out_weight,
    state_cache,
    stretch_len,
    stretch_slot,
    decode_slot,
    decode_owner,
):
    head_count = qkv_weight.shape[1]
    block_width = qkv_weight.shape[2]
    rows_own = stretch_tokens.shape[1]
    w_flat = qkv_weight.reshape(D, head_count * block_width)
    gains = out_gain.reshape(head_count, DH)
    normed = rms_rows(stretch_tokens[0], norm_gain).astype(jnp.bfloat16)
    rim_rows = from_behind(normed[rows_own - 2 :], "head", 1)
    first_dev = lax.axis_index("head") == 0
    rim_rows = jnp.where(first_dev, stretch_tail[0], rim_rows)
    conved = convolve(rim_rows, normed, conv_taps)
    dec_normed = rms_rows(decode_tokens[0], norm_gain).astype(jnp.bfloat16)
    dec_conved = convolve(decode_tail[0], dec_normed[:, None, :], conv_taps)[:, 0, :]
    dec_qkv = jnp.dot(dec_conved, w_flat, preferred_element_type=jnp.float32).astype(jnp.bfloat16)
    owners = decode_owner[0, :, 0]
    slots_here = decode_slot[0]
    groups = lax.axis_size("tok")
    capacity = max(2, 2 * DEC // groups)
    earlier = jnp.arange(DEC)[None, :] < jnp.arange(DEC)[:, None]
    same_owner = owners[None, :] == owners[:, None]
    rank_in = jnp.sum(earlier & same_owner, axis=1)
    target = owners * capacity + rank_in
    placing = jnp.arange(groups * capacity)[:, None] == target[None, :]
    sent_rows = jnp.dot(placing.astype(jnp.bfloat16), dec_qkv, preferred_element_type=jnp.float32)
    sent_slots = jnp.sum(jnp.where(placing, slots_here[None, :] + 1, 0), axis=1) - 1
    wide = head_count * block_width
    sent = jnp.concatenate([sent_rows, sent_slots[:, None].astype(jnp.float32)], axis=1)
    sent = sent.reshape(groups, capacity * (wide + 1))
    lines = -(-sent.shape[1] // 1024) * 8
    sent = jnp.pad(sent, ((0, 0), (0, lines * 128 - sent.shape[1]))).reshape(groups, lines, 128)
    grouped, items = gather_project(conved, w_flat, sent)
    grouped = grouped.reshape(STRETCH, head_count, block_width)
    queries = grouped[:, :, :F]
    key_feats = grouped[:, :, F : 2 * F]
    values = grouped[:, :, 2 * F :]
    length = stretch_len[0]
    positions = jnp.arange(STRETCH)
    valid_rows = positions < length
    state_old = lax.dynamic_index_in_dim(state_cache[0], stretch_slot[0], 0, keepdims=False)
    carried = jnp.einsum(
        "ihp,hdp->ihd",
        features(queries.astype(jnp.float32)),
        state_old,
        precision=lax.Precision.HIGHEST,
    )
    block_rows = min(512, STRETCH)
    pieces = []
    for anchor in range(0, STRETCH, block_rows):
        finish = anchor + block_rows
        inner = jnp.einsum(
            "ihf,jhf->hij",
            queries[anchor:finish],
            key_feats[:finish],
            preferred_element_type=jnp.float32,
        ) / math.sqrt(F)
        weights = 1.0 + inner + 0.5 * inner * inner
        allowed = (positions[None, :finish] <= positions[anchor:finish, None]) & valid_rows[
            None, :finish
        ]
        weights = jnp.where(allowed[None], weights, 0.0).astype(jnp.bfloat16)
        pieces.append(
            jnp.einsum("hij,jhd->ihd", weights, values[:finish], preferred_element_type=jnp.float32)
        )
    local_sum = jnp.concatenate(pieces, axis=0)
    attended = rms_rows(carried + local_sum, gains)
    attended = (
        jnp.where(valid_rows[:, None, None], attended, 0.0)
        .astype(jnp.bfloat16)
        .reshape(STRETCH, head_count * DH)
    )
    key_phi = jnp.where(
        valid_rows[:, None, None], features(key_feats.astype(jnp.float32)), 0.0
    ).astype(jnp.bfloat16)
    state_next = state_old + jnp.einsum(
        "jhd,jhp->hdp", values, key_phi, preferred_element_type=jnp.float32
    )
    items = items.reshape(groups, lines * 128)[:, : capacity * (wide + 1)]
    items = items.reshape(groups * capacity, wide + 1)
    served = decode_items(
        items[:, :wide], items[:, wide].astype(jnp.int32), state_cache[0], out_gain, head_count
    )
    served = served.astype(jnp.float32).reshape(groups, capacity, head_count * DH)
    served = jnp.pad(served, ((0, 0), (0, 8 - capacity), (0, 128 - head_count * DH)))
    heads = lax.axis_size("head")
    per_head = DEC // heads
    spots = (owners * 8 + rank_in).reshape(heads, per_head).T.reshape(DEC)
    putting = (spots[:, None] == jnp.arange(groups * 8)[None, :]).astype(jnp.bfloat16)
    stretch_out, dec_sum = project_scatter(attended, out_weight, served, putting)
    dec_sum = dec_sum[: per_head * D // 128].reshape(D // 128, per_head, 128)
    decode_out = jnp.transpose(dec_sum, (1, 0, 2)).reshape(per_head, D)
    return (stretch_out[None], decode_out[None], state_next[None])


def solution(mesh):
    in_specs = (
        P("tok", "head", None),
        P("tok", None, None),
        P("tok", None, None),
        P("tok", None, None, None),
        P(),
        P(),
        P(None, "head", None),
        P("head"),
        P("head", None),
        P("tok", None, "head", None, None),
        P("tok"),
        P("tok"),
        P("tok", None),
        P("tok", None, None),
    )
    out_specs = (P("tok", "head", None), P("tok", "head", None), P("tok", "head", None, None))
    return jax.shard_map(local, mesh=mesh, in_specs=in_specs, out_specs=out_specs, check_vma=False)
```

```python
import functools
import math

import jax
import jax.numpy as jnp
from jax import lax
from jax.experimental import pallas as pl
from jax.experimental.pallas import tpu as pltpu
from jax.sharding import PartitionSpec as P

D = 1792
DH = 112
F = 16
STRETCH = 1024
DEC = 32


SIDE = 4
MESH = pl.DeviceIdType.MESH


def plane_position():
    me = lax.axis_index("head")
    return me, lax.rem(me, SIDE), lax.div(me, SIDE)


def block_at(half, first, second, mx, my):
    dx, dy = (first, second) if half == 0 else (second, first)
    return lax.rem(my + dy % SIDE, SIDE) * SIDE + lax.rem(mx + dx % SIDE, SIDE)


def half_rows(half, quarter, rows):
    start = half * (rows // 2)
    if quarter is None:
        return pl.ds(start, rows // 2)
    return pl.ds(start + quarter * (rows // 4), rows // 4)


def greet(peers):
    barrier = pltpu.get_barrier_semaphore()
    for peer in peers:
        pl.semaphore_signal(barrier, inc=1, device_id={"head": peer}, device_id_type=MESH)
    groups, mine = lax.axis_size("tok"), lax.axis_index("tok")

    def hail(k, carry):
        pl.semaphore_signal(
            barrier, inc=1, device_id={"tok": lax.rem(mine + k, groups)}, device_id_type=MESH
        )
        return carry

    lax.fori_loop(1, groups, hail, 0)
    return barrier, len(peers) + groups - 1


def swap_copy(k, source, landing, send_sem, recv_sem):
    groups, mine = lax.axis_size("tok"), lax.axis_index("tok")
    peer = lax.rem(mine + k, groups)
    return pltpu.make_async_remote_copy(
        src_ref=source.at[peer],
        dst_ref=landing.at[mine],
        send_sem=send_sem.at[k],
        recv_sem=recv_sem.at[k],
        device_id={"tok": peer},
        device_id_type=MESH,
    )


def swap_start(source, landing, send_sem, recv_sem):
    def body(k, carry):
        swap_copy(k, source, landing, send_sem, recv_sem).start()
        return carry

    lax.fori_loop(1, lax.axis_size("tok"), body, 0)


def swap_finish(source, landing, send_sem, recv_sem):
    groups, mine = lax.axis_size("tok"), lax.axis_index("tok")

    def body(k, carry):
        origin = lax.rem(mine + groups - k, groups)
        pltpu.make_async_remote_copy(
            src_ref=landing.at[origin],
            dst_ref=landing.at[origin],
            send_sem=send_sem.at[k],
            recv_sem=recv_sem.at[k],
            device_id={"tok": lax.rem(mine + k, groups)},
            device_id_type=MESH,
        ).wait_recv()
        swap_copy(k, source, landing, send_sem, recv_sem).wait_send()
        return carry

    lax.fori_loop(1, groups, body, 0)
    landing[mine] = source[mine]


def gather_kernel(
    own_ref, w_ref, tokens_ref, tails_ref, gain_ref, taps_ref, put_ref, slot_ref, qkv_ref, got_ref,
    buf, items_ref, landing, send_sem, recv_sem, swap_send, swap_recv,
):
    me, mx, my = plane_position()
    rows = own_ref.shape[0]
    barrier, callers = greet(
        [block_at(0, d, 0, mx, my) for d in (1, -1)] + [block_at(0, 0, d, mx, my) for d in (1, -1)]
    )
    sent = []

    def send(half, first, second, along_first, step, quarter=None):
        target = block_at(half, step if along_first else 0, 0 if along_first else step, mx, my)
        there = ((first - step) % SIDE, second) if along_first else (first, (second - step) % SIDE)
        block = block_at(half, first, second, mx, my)
        span = half_rows(half, quarter, rows)
        own = first == 0 and second == 0
        slot = half * 16 + there[0] * SIDE + there[1]
        copy = pltpu.make_async_remote_copy(
            src_ref=own_ref.at[span] if own else buf.at[block, span],
            dst_ref=buf.at[block, span],
            send_sem=send_sem.at[len(sent)],
            recv_sem=recv_sem.at[slot, quarter or 0],
            device_id={"head": target},
            device_id_type=MESH,
        )
        copy.start()
        sent.append(copy)

    def arrived(half, first, second, quarter=None):
        first, second = first % SIDE, second % SIDE
        place = buf.at[block_at(half, first, second, mx, my), half_rows(half, quarter, rows)]
        pltpu.make_async_remote_copy(
            src_ref=place,
            dst_ref=place,
            send_sem=send_sem.at[0],
            recv_sem=recv_sem.at[half * 16 + first * SIDE + second, quarter or 0],
            device_id={"head": block_at(0, 1, 0, mx, my)},
            device_id_type=MESH,
        ).wait_recv()

    def project(block, value):
        product = jnp.dot(value, w_ref[...], preferred_element_type=jnp.float32)
        qkv_ref[pl.ds(pl.multiple_of(block * rows, rows), rows), :] = product.astype(jnp.bfloat16)

    normed = rms_rows(tokens_ref[...], gain_ref[...]).astype(jnp.bfloat16).astype(jnp.float32)
    width = own_ref.shape[1]
    total = taps_ref[0:1, :] * tails_ref[:, :width].astype(jnp.float32)
    total = total + taps_ref[1:2, :] * tails_ref[:, width:].astype(jnp.float32)
    total = (total + taps_ref[2:3, :] * normed).astype(jnp.bfloat16)
    dec_qkv = jnp.dot(total, w_ref[...], preferred_element_type=jnp.float32).astype(jnp.bfloat16)
    placed = jnp.dot(put_ref[...], dec_qkv, preferred_element_type=jnp.float32) + slot_ref[...]
    items_ref[...] = jnp.zeros(items_ref.shape, jnp.float32)
    items_ref[:, :, : w_ref.shape[1]] = placed.reshape(items_ref.shape[:2] + (w_ref.shape[1],))
    project(me, own_ref[...])
    pl.semaphore_wait(barrier, callers)
    for along_first in (False, True):
        for half in (0, 1):
            for step in (1, -1):
                send(half, 0, 0, along_first, step)
    swap_start(items_ref, landing, swap_send, swap_recv)
    for step in (1, -1):
        for half in (0, 1):
            origin = -step % SIDE
            arrived(half, origin, 0)
            send(half, origin, 0, True, step, 0 if step == 1 else 1)
            for out in (1, -1):
                send(half, origin, 0, False, out)

    def pass_on(half, first):
        for step in (1, -1):
            origin = -step % SIDE
            arrived(half, first, origin)
            send(half, first, origin, False, step, 0 if step == 1 else 1)

    for half in (0, 1):
        pass_on(half, 0)
    for half in (0, 1):
        for quarter in (0, 1):
            arrived(half, 2, 0, quarter)
        for out in (1, -1):
            send(half, 2, 0, False, out)
    for first in (3, 1, 2):
        for half in (0, 1):
            pass_on(half, first)
    swap_finish(items_ref, landing, swap_send, swap_recv)
    got_ref[...] = landing[...]
    for dx in (1, 3, 0):
        for dy in (1, 3, 0):
            if dx or dy:
                block = block_at(0, dx, dy, mx, my)
                project(block, buf[block])
    for first in (0, 3, 1, 2):
        for half in (0, 1):
            for quarter in (0, 1):
                arrived(half, first, 2, quarter)
        for dx, dy in {(first, 2), (2, first)}:
            block = block_at(0, dx, dy, mx, my)
            project(block, buf[block])
    for copy in sent:
        copy.wait_send()


def gather_project(conved, weight, tokens, tails, gain, taps, putting, slots):
    rows, width = conved.shape
    columns = weight.shape[1]
    swapped = (putting.shape[0] // 8, 8, -(-columns // 128) * 128)
    whole = pl.BlockSpec(memory_space=pltpu.VMEM)
    return pl.pallas_call(
        gather_kernel,
        out_shape=(
            jax.ShapeDtypeStruct((16 * rows, columns), jnp.bfloat16),
            jax.ShapeDtypeStruct(swapped, jnp.float32),
        ),
        in_specs=[whole] * 8,
        out_specs=(whole, whole),
        scratch_shapes=[
            pltpu.VMEM((16, rows, width), jnp.bfloat16),
            pltpu.VMEM(swapped, jnp.float32),
            pltpu.VMEM(swapped, jnp.float32),
            pltpu.SemaphoreType.DMA((40,)),
            pltpu.SemaphoreType.DMA((32, 2)),
            pltpu.SemaphoreType.DMA((swapped[0],)),
            pltpu.SemaphoreType.DMA((swapped[0],)),
        ],
        compiler_params=pltpu.CompilerParams(
            collective_id=0, has_side_effects=True, vmem_limit_bytes=40 * 2**20
        ),
        name="gather_project",
    )(conved, weight, tokens, tails, gain, taps, putting, slots)


def scatter_kernel(
    rows, att_ref, w_ref, served_ref, place_ref, out_ref, dec_out_ref,
    part, far, near, far_last, near_last, landing, dec_wide, dec_ref, dec_in,
    send_sem, far_sem, near_sem, dec_send, dec_recv, swap_send, swap_recv,
):
    me, mx, my = plane_position()
    peers = [lax.rem(me + k, 16) for k in range(1, 16)]
    barrier, callers = greet(peers)
    sent = []

    def send(half, along_first, step, source, target_ref, sem):
        copy = pltpu.make_async_remote_copy(
            src_ref=source,
            dst_ref=target_ref,
            send_sem=send_sem.at[len(sent)],
            recv_sem=sem,
            device_id={
                "head": block_at(half, step if along_first else 0, 0 if along_first else step, mx, my)
            },
            device_id_type=MESH,
        )
        copy.start()
        sent.append(copy)

    def arrived(place, sem):
        pltpu.make_async_remote_copy(
            src_ref=place,
            dst_ref=place,
            send_sem=send_sem.at[0],
            recv_sem=sem,
            device_id={"head": block_at(0, 1, 0, mx, my)},
            device_id_type=MESH,
        ).wait_recv()

    def project(dx, dy):
        block = block_at(0, dx, dy, mx, my)
        value = att_ref[pl.ds(pl.multiple_of(block * rows, rows), rows), :]
        product = jnp.dot(value, w_ref[...], preferred_element_type=jnp.float32)
        part[block] = product.astype(jnp.bfloat16)

    def piece(half, first, second, quarter=None):
        return block_at(half, first, second, mx, my), half_rows(half, quarter, rows)

    def wide(value):
        return value.astype(jnp.float32)

    def send_far(half, first):
        for quarter, step in ((0, -1), (1, 1)):
            block, span = piece(half, first, 2, quarter)
            slot = half * SIDE + first
            send(half, False, step, part.at[block, span], far.at[slot, quarter], far_sem.at[slot, quarter])

    order = (2, 1, 3, 0)
    for first in order:
        for dx, dy in sorted({(first, 2), (2, first)}):
            project(dx, dy)
    for dx, dy in ((1, 1), (1, 3), (3, 1), (3, 3), (0, 1), (1, 0)):
        project(dx, dy)
    pl.semaphore_wait(barrier, callers)
    for first in order:
        for half in (0, 1):
            send_far(half, first)
    swap_start(served_ref, landing, swap_send, swap_recv)
    for dx, dy in ((3, 0), (0, 3), (0, 0)):
        project(dx, dy)
    for first in order:
        for half in (0, 1):
            slot = half * SIDE + first
            for quarter, step in ((0, -1), (1, 1)):
                arrived(far.at[slot, quarter], far_sem.at[slot, quarter])
                block, span = piece(half, first, step, quarter)
                part[block, span, :] = (wide(part[block, span, :]) + wide(far[slot, quarter])).astype(jnp.bfloat16)
                block, span = piece(half, first, step)
                send(half, False, step, part.at[block, span], near.at[slot, quarter], near_sem.at[slot, quarter])
    swap_finish(served_ref, landing, swap_send, swap_recv)
    groups, item_rows, lanes = landing.shape
    returned = landing[...].reshape(groups * item_rows, lanes).astype(jnp.bfloat16)
    dec_att = jnp.dot(place_ref[...], returned, preferred_element_type=jnp.float32)
    dec_att = dec_att.astype(jnp.bfloat16)[:, : w_ref.shape[0]]
    dec_part = jnp.dot(dec_att, w_ref[...], preferred_element_type=jnp.float32)
    dec_wide[...] = jnp.zeros(dec_wide.shape, jnp.float32)
    per_peer = dec_part.shape[0] // 16
    for chunk in range(dec_part.shape[1] // lanes):
        for row in range(per_peer):
            dec_wide[:, chunk * per_peer + row, :] = dec_part[
                row * 16 : row * 16 + 16, chunk * lanes : (chunk + 1) * lanes
            ]
    dec_ref[...] = dec_wide[...].astype(jnp.bfloat16)
    dec_copies = []
    for k, peer in enumerate(peers):
        copy = pltpu.make_async_remote_copy(
            src_ref=dec_ref.at[peer],
            dst_ref=dec_in.at[k],
            send_sem=dec_send.at[k],
            recv_sem=dec_recv.at[k],
            device_id={"head": peer},
            device_id_type=MESH,
        )
        copy.start()
        dec_copies.append(copy)
    for first in order:
        for half in (0, 1):
            slot = half * SIDE + first
            for quarter in (0, 1):
                arrived(near.at[slot, quarter], near_sem.at[slot, quarter])
            block, span = piece(half, first, 0)
            if first == 0:
                continue
            total = wide(part[block, span, :]) + wide(near[slot, 0]) + wide(near[slot, 1])
            part[block, span, :] = total.astype(jnp.bfloat16)
            if first == 2:
                for quarter, step in ((0, -1), (1, 1)):
                    block, span = piece(half, 2, 0, quarter)
                    send(half, True, step, part.at[block, span], far_last.at[half, quarter], far_sem.at[8 + half, quarter])
            else:
                quarter, step = (1, 1) if first == 1 else (0, -1)
                arrived(far_last.at[half, quarter], far_sem.at[8 + half, quarter])
                inner, inner_span = piece(half, step, 0, quarter)
                part[inner, inner_span, :] = (
                    wide(part[inner, inner_span, :]) + wide(far_last[half, quarter])
                ).astype(jnp.bfloat16)
                send(half, True, step, part.at[block, span], near_last.at[half, quarter], near_sem.at[8 + half, quarter])
    dec_total = wide(dec_ref[me])
    for k, copy in enumerate(dec_copies):
        copy.wait_recv()
        dec_total = dec_total + wide(dec_in[k])
    dec_out_ref[...] = dec_total.astype(jnp.bfloat16)
    for half in (0, 1):
        block, span = piece(half, 0, 0)
        total = wide(part[block, span, :]) + wide(near[half * SIDE, 0]) + wide(near[half * SIDE, 1])
        for quarter in (0, 1):
            arrived(near_last.at[half, quarter], near_sem.at[8 + half, quarter])
            total = total + wide(near_last[half, quarter])
        out_ref[span, :] = total.astype(jnp.bfloat16)
    for copy in sent:
        copy.wait_send()
    for copy in dec_copies:
        copy.wait_send()


def project_scatter(attended, weight, served, placing):
    rows = attended.shape[0] // 16
    width = weight.shape[1]
    lanes = served.shape[2]
    dec_rows = -(-placing.shape[0] // 16 * width // lanes // 16) * 16
    whole = pl.BlockSpec(memory_space=pltpu.VMEM)
    return pl.pallas_call(
        functools.partial(scatter_kernel, rows),
        out_shape=(
            jax.ShapeDtypeStruct((rows, width), jnp.bfloat16),
            jax.ShapeDtypeStruct((dec_rows, lanes), jnp.bfloat16),
        ),
        in_specs=[whole, whole, whole, whole],
        out_specs=(whole, whole),
        scratch_shapes=[
            pltpu.VMEM((16, rows, width), jnp.bfloat16),
            pltpu.VMEM((8, 2, rows // 4, width), jnp.bfloat16),
            pltpu.VMEM((8, 2, rows // 2, width), jnp.bfloat16),
            pltpu.VMEM((2, 2, rows // 4, width), jnp.bfloat16),
            pltpu.VMEM((2, 2, rows // 2, width), jnp.bfloat16),
            pltpu.VMEM(served.shape, served.dtype),
            pltpu.VMEM((16, dec_rows, lanes), jnp.float32),
            pltpu.VMEM((16, dec_rows, lanes), jnp.bfloat16),
            pltpu.VMEM((15, dec_rows, lanes), jnp.bfloat16),
            pltpu.SemaphoreType.DMA((40,)),
            pltpu.SemaphoreType.DMA((10, 2)),
            pltpu.SemaphoreType.DMA((10, 2)),
            pltpu.SemaphoreType.DMA((15,)),
            pltpu.SemaphoreType.DMA((15,)),
            pltpu.SemaphoreType.DMA((served.shape[0],)),
            pltpu.SemaphoreType.DMA((served.shape[0],)),
        ],
        compiler_params=pltpu.CompilerParams(
            collective_id=1, has_side_effects=True, vmem_limit_bytes=40 * 2**20
        ),
        name="project_scatter",
    )(attended, weight, served, placing)


def from_behind(array, axis, by):
    peers = lax.axis_size(axis)
    pairs = [(i, i + by) for i in range(peers) if 0 <= i + by < peers]
    return lax.ppermute(array, axis, pairs)


def rms_rows(values, gain):
    values = values.astype(jnp.float32)
    factor = lax.rsqrt(jnp.mean(values * values, axis=-1, keepdims=True) + 1e-05)
    return values * factor * gain


def features(vectors):
    breadth = vectors.shape[-1]
    linear = vectors / math.sqrt(math.sqrt(breadth))
    index = jnp.arange(breadth * breadth)[None, :]
    which = jnp.arange(breadth)[:, None]
    slow = (index // breadth == which).astype(jnp.bfloat16)
    fast = (index % breadth == which).astype(jnp.bfloat16)
    exact = vectors.astype(jnp.bfloat16)
    outer = jnp.dot(exact, slow, preferred_element_type=jnp.float32) * jnp.dot(
        exact, fast, preferred_element_type=jnp.float32
    )
    outer = outer / math.sqrt(2.0 * breadth)
    ones = jnp.ones(vectors.shape[:-1] + (1,), vectors.dtype)
    return jnp.concatenate([ones, linear, outer], axis=-1)


def convolve(tail, normed, conv_taps):
    joined = jnp.concatenate([tail, normed], axis=-2).astype(jnp.float32)
    span_rows = normed.shape[-2]
    total = conv_taps[0] * joined[..., 0:span_rows, :]
    total = total + conv_taps[1] * joined[..., 1 : span_rows + 1, :]
    total = total + conv_taps[2] * joined[..., 2 : span_rows + 2, :]
    return total.astype(jnp.bfloat16)


def decode_items(items, slot_items, cache_own, out_gain, head_count):
    item_count = items.shape[0]
    shaped = items.reshape(item_count, head_count, 2 * F + DH).astype(jnp.float32)
    queries = shaped[:, :, :F]
    key_feats = shaped[:, :, F : 2 * F]
    values = shaped[:, :, 2 * F :]
    slot_total = cache_own.shape[0]
    table = jnp.einsum(
        "nhp,shdp->nshd", features(queries), cache_own, precision=lax.Precision.HIGHEST
    )
    picker = (slot_items[:, None] == jnp.arange(slot_total)[None, :]).astype(jnp.float32)
    carried = jnp.einsum("ns,nshd->nhd", picker, table, precision=lax.Precision.HIGHEST)
    inner = jnp.sum(queries * key_feats, axis=-1) / math.sqrt(F)
    own_term = (1.0 + inner + 0.5 * inner * inner)[..., None] * values
    attended = rms_rows(carried + own_term, out_gain.reshape(head_count, DH))
    return attended.astype(jnp.bfloat16).reshape(item_count, head_count * DH)


def local(
    stretch_tokens,
    stretch_tail,
    decode_tokens,
    decode_tail,
    norm_gain,
    conv_taps,
    qkv_weight,
    out_gain,
    out_weight,
    state_cache,
    stretch_len,
    stretch_slot,
    decode_slot,
    decode_owner,
):
    head_count = qkv_weight.shape[1]
    block_width = qkv_weight.shape[2]
    rows_own = stretch_tokens.shape[1]
    w_flat = qkv_weight.reshape(D, head_count * block_width)
    gains = out_gain.reshape(head_count, DH)
    normed = rms_rows(stretch_tokens[0], norm_gain).astype(jnp.bfloat16)
    rim_rows = from_behind(normed[rows_own - 2 :], "head", 1)
    first_dev = lax.axis_index("head") == 0
    rim_rows = jnp.where(first_dev, stretch_tail[0], rim_rows)
    conved = convolve(rim_rows, normed, conv_taps)
    owners = decode_owner[0, :, 0]
    slots_here = decode_slot[0]
    groups = lax.axis_size("tok")
    capacity = max(2, 2 * DEC // groups)
    earlier = jnp.arange(DEC)[None, :] < jnp.arange(DEC)[:, None]
    same_owner = owners[None, :] == owners[:, None]
    rank_in = jnp.sum(earlier & same_owner, axis=1)
    spots = owners * 8 + rank_in
    lines = jnp.arange(groups * 8)
    gathering = (lines[:, None] == spots[None, :]).astype(jnp.bfloat16)
    named = lines[:, None] == spots[None, :] + capacity
    slot_column = jnp.sum(jnp.where(named, slots_here[None, :], 0), axis=1, keepdims=True)
    grouped, items = gather_project(
        conved, w_flat, decode_tokens[0], decode_tail[0].reshape(DEC, 2 * D), norm_gain[None],
        conv_taps, gathering, slot_column.astype(jnp.float32),
    )
    grouped = grouped.reshape(STRETCH, head_count, block_width)
    queries = grouped[:, :, :F]
    key_feats = grouped[:, :, F : 2 * F]
    values = grouped[:, :, 2 * F :]
    length = stretch_len[0]
    positions = jnp.arange(STRETCH)
    valid_rows = positions < length
    state_old = lax.dynamic_index_in_dim(state_cache[0], stretch_slot[0], 0, keepdims=False)
    carried = jnp.einsum(
        "ihp,hdp->ihd",
        features(queries.astype(jnp.float32)),
        state_old,
        precision=lax.Precision.HIGHEST,
    )
    block_rows = min(512, STRETCH)
    pieces = []
    for anchor in range(0, STRETCH, block_rows):
        finish = anchor + block_rows
        inner = jnp.einsum(
            "ihf,jhf->hij",
            queries[anchor:finish],
            key_feats[:finish],
            preferred_element_type=jnp.float32,
        ) / math.sqrt(F)
        weights = 1.0 + inner + 0.5 * inner * inner
        allowed = (positions[None, :finish] <= positions[anchor:finish, None]) & valid_rows[
            None, :finish
        ]
        weights = jnp.where(allowed[None], weights, 0.0).astype(jnp.bfloat16)
        pieces.append(
            jnp.einsum("hij,jhd->ihd", weights, values[:finish], preferred_element_type=jnp.float32)
        )
    local_sum = jnp.concatenate(pieces, axis=0)
    attended = rms_rows(carried + local_sum, gains)
    attended = (
        jnp.where(valid_rows[:, None, None], attended, 0.0)
        .astype(jnp.bfloat16)
        .reshape(STRETCH, head_count * DH)
    )
    key_phi = jnp.where(
        valid_rows[:, None, None], features(key_feats.astype(jnp.float32)), 0.0
    ).astype(jnp.bfloat16)
    state_next = state_old + jnp.einsum(
        "jhd,jhp->hdp", values, key_phi, preferred_element_type=jnp.float32
    )
    wide = head_count * block_width
    item_rows = items[:, :capacity, :wide].reshape(groups * capacity, wide)
    item_slots = items[:, capacity : 2 * capacity, 0].reshape(groups * capacity)
    served = decode_items(
        item_rows, item_slots.astype(jnp.int32), state_cache[0], out_gain, head_count
    )
    served = served.astype(jnp.float32).reshape(groups, capacity, head_count * DH)
    served = jnp.pad(served, ((0, 0), (0, 8 - capacity), (0, 128 - head_count * DH)))
    heads = lax.axis_size("head")
    per_head = DEC // heads
    returns = spots.reshape(heads, per_head).T.reshape(DEC)
    putting = (returns[:, None] == jnp.arange(groups * 8)[None, :]).astype(jnp.bfloat16)
    stretch_out, dec_sum = project_scatter(attended, out_weight, served, putting)
    dec_sum = dec_sum[: per_head * D // 128].reshape(D // 128, per_head, 128)
    decode_out = jnp.transpose(dec_sum, (1, 0, 2)).reshape(per_head, D)
    return (stretch_out[None], decode_out[None], state_next[None])


def solution(mesh):
    in_specs = (
        P("tok", "head", None),
        P("tok", None, None),
        P("tok", None, None),
        P("tok", None, None, None),
        P(),
        P(),
        P(None, "head", None),
        P("head"),
        P("head", None),
        P("tok", None, "head", None, None),
        P("tok"),
        P("tok"),
        P("tok", None),
        P("tok", None, None),
    )
    out_specs = (P("tok", "head", None), P("tok", "head", None), P("tok", "head", None, None))
    return jax.shard_map(local, mesh=mesh, in_specs=in_specs, out_specs=out_specs, check_vma=False)
```

```python
import functools
import math

import jax
import jax.numpy as jnp
from jax import lax
from jax.experimental import pallas as pl
from jax.experimental.pallas import tpu as pltpu
from jax.sharding import PartitionSpec as P

D = 1792
DH = 112
F = 16
STRETCH = 1024
DEC = 32


SIDE = 4
MESH = pl.DeviceIdType.MESH


def plane_position():
    me = lax.axis_index("head")
    return me, lax.rem(me, SIDE), lax.div(me, SIDE)


def block_at(half, first, second, mx, my):
    dx, dy = (first, second) if half == 0 else (second, first)
    return lax.rem(my + dy % SIDE, SIDE) * SIDE + lax.rem(mx + dx % SIDE, SIDE)


def half_rows(half, quarter, rows):
    start = half * (rows // 2)
    if quarter is None:
        return pl.ds(start, rows // 2)
    return pl.ds(start + quarter * (rows // 4), rows // 4)


def greet(peers):
    barrier = pltpu.get_barrier_semaphore()
    for peer in peers:
        pl.semaphore_signal(barrier, inc=1, device_id={"head": peer}, device_id_type=MESH)
    groups, mine = lax.axis_size("tok"), lax.axis_index("tok")

    def hail(k, carry):
        pl.semaphore_signal(
            barrier, inc=1, device_id={"tok": lax.rem(mine + k, groups)}, device_id_type=MESH
        )
        return carry

    lax.fori_loop(1, groups, hail, 0)
    return barrier, len(peers) + groups - 1


def swap_copy(k, source, landing, send_sem, recv_sem):
    groups, mine = lax.axis_size("tok"), lax.axis_index("tok")
    peer = lax.rem(mine + k, groups)
    return pltpu.make_async_remote_copy(
        src_ref=source.at[peer],
        dst_ref=landing.at[mine],
        send_sem=send_sem.at[k],
        recv_sem=recv_sem.at[k],
        device_id={"tok": peer},
        device_id_type=MESH,
    )


def swap_start(source, landing, send_sem, recv_sem):
    def body(k, carry):
        swap_copy(k, source, landing, send_sem, recv_sem).start()
        return carry

    lax.fori_loop(1, lax.axis_size("tok"), body, 0)


def swap_finish(source, landing, send_sem, recv_sem):
    groups, mine = lax.axis_size("tok"), lax.axis_index("tok")

    def body(k, carry):
        origin = lax.rem(mine + groups - k, groups)
        pltpu.make_async_remote_copy(
            src_ref=landing.at[origin],
            dst_ref=landing.at[origin],
            send_sem=send_sem.at[k],
            recv_sem=recv_sem.at[k],
            device_id={"tok": lax.rem(mine + k, groups)},
            device_id_type=MESH,
        ).wait_recv()
        swap_copy(k, source, landing, send_sem, recv_sem).wait_send()
        return carry

    lax.fori_loop(1, groups, body, 0)
    landing[mine] = source[mine]


def gather_kernel(
    own_ref, w_ref, tokens_ref, tails_ref, gain_ref, taps_ref, put_ref, slot_ref, qkv_ref, got_ref,
    buf, items_ref, landing, send_sem, recv_sem, swap_send, swap_recv,
):
    me, mx, my = plane_position()
    rows = own_ref.shape[0]
    barrier, callers = greet(
        [block_at(0, d, 0, mx, my) for d in (1, -1)] + [block_at(0, 0, d, mx, my) for d in (1, -1)]
    )
    sent = []

    def send(half, first, second, along_first, step, quarter=None):
        target = block_at(half, step if along_first else 0, 0 if along_first else step, mx, my)
        there = ((first - step) % SIDE, second) if along_first else (first, (second - step) % SIDE)
        block = block_at(half, first, second, mx, my)
        span = half_rows(half, quarter, rows)
        own = first == 0 and second == 0
        slot = half * 16 + there[0] * SIDE + there[1]
        copy = pltpu.make_async_remote_copy(
            src_ref=own_ref.at[span] if own else buf.at[block, span],
            dst_ref=buf.at[block, span],
            send_sem=send_sem.at[len(sent)],
            recv_sem=recv_sem.at[slot, quarter or 0],
            device_id={"head": target},
            device_id_type=MESH,
        )
        copy.start()
        sent.append(copy)

    def arrived(half, first, second, quarter=None):
        first, second = first % SIDE, second % SIDE
        place = buf.at[block_at(half, first, second, mx, my), half_rows(half, quarter, rows)]
        pltpu.make_async_remote_copy(
            src_ref=place,
            dst_ref=place,
            send_sem=send_sem.at[0],
            recv_sem=recv_sem.at[half * 16 + first * SIDE + second, quarter or 0],
            device_id={"head": block_at(0, 1, 0, mx, my)},
            device_id_type=MESH,
        ).wait_recv()

    def project(block, value):
        product = jnp.dot(value, w_ref[...], preferred_element_type=jnp.float32)
        qkv_ref[pl.ds(pl.multiple_of(block * rows, rows), rows), :] = product.astype(jnp.bfloat16)

    normed = rms_rows(tokens_ref[...], gain_ref[...][None, :]).astype(jnp.bfloat16).astype(jnp.float32)
    width = own_ref.shape[1]
    total = taps_ref[0:1, :] * tails_ref[:, :width].astype(jnp.float32)
    total = total + taps_ref[1:2, :] * tails_ref[:, width:].astype(jnp.float32)
    total = (total + taps_ref[2:3, :] * normed).astype(jnp.bfloat16)
    dec_qkv = jnp.dot(total, w_ref[...], preferred_element_type=jnp.float32).astype(jnp.bfloat16)
    placed = jnp.dot(put_ref[...], dec_qkv, preferred_element_type=jnp.float32) + slot_ref[...]
    items_ref[...] = jnp.zeros(items_ref.shape, jnp.float32)
    items_ref[:, :, : w_ref.shape[1]] = placed.reshape(items_ref.shape[:2] + (w_ref.shape[1],))
    project(me, own_ref[...])
    pl.semaphore_wait(barrier, callers)
    for along_first in (False, True):
        for half in (0, 1):
            for step in (1, -1):
                send(half, 0, 0, along_first, step)
    swap_start(items_ref, landing, swap_send, swap_recv)
    for step in (1, -1):
        for half in (0, 1):
            origin = -step % SIDE
            arrived(half, origin, 0)
            send(half, origin, 0, True, step, 0 if step == 1 else 1)
            for out in (1, -1):
                send(half, origin, 0, False, out)

    def pass_on(half, first):
        for step in (1, -1):
            origin = -step % SIDE
            arrived(half, first, origin)
            send(half, first, origin, False, step, 0 if step == 1 else 1)

    for half in (0, 1):
        pass_on(half, 0)
    for half in (0, 1):
        for quarter in (0, 1):
            arrived(half, 2, 0, quarter)
        for out in (1, -1):
            send(half, 2, 0, False, out)
    for first in (3, 1, 2):
        for half in (0, 1):
            pass_on(half, first)
    swap_finish(items_ref, landing, swap_send, swap_recv)
    got_ref[...] = landing[...]
    for dx in (1, 3, 0):
        for dy in (1, 3, 0):
            if dx or dy:
                block = block_at(0, dx, dy, mx, my)
                project(block, buf[block])
    for first in (0, 3, 1, 2):
        for half in (0, 1):
            for quarter in (0, 1):
                arrived(half, first, 2, quarter)
        for dx, dy in {(first, 2), (2, first)}:
            block = block_at(0, dx, dy, mx, my)
            project(block, buf[block])
    for copy in sent:
        copy.wait_send()


def gather_project(conved, weight, tokens, tails, gain, taps, putting, slots):
    rows, width = conved.shape
    columns = weight.shape[1]
    swapped = (putting.shape[0] // 8, 8, -(-columns // 128) * 128)
    whole = pl.BlockSpec(memory_space=pltpu.VMEM)
    return pl.pallas_call(
        gather_kernel,
        out_shape=(
            jax.ShapeDtypeStruct((16 * rows, columns), jnp.bfloat16),
            jax.ShapeDtypeStruct(swapped, jnp.float32),
        ),
        in_specs=[whole] * 8,
        out_specs=(whole, whole),
        scratch_shapes=[
            pltpu.VMEM((16, rows, width), jnp.bfloat16),
            pltpu.VMEM(swapped, jnp.float32),
            pltpu.VMEM(swapped, jnp.float32),
            pltpu.SemaphoreType.DMA((40,)),
            pltpu.SemaphoreType.DMA((32, 2)),
            pltpu.SemaphoreType.DMA((swapped[0],)),
            pltpu.SemaphoreType.DMA((swapped[0],)),
        ],
        compiler_params=pltpu.CompilerParams(
            collective_id=0, has_side_effects=True, vmem_limit_bytes=40 * 2**20
        ),
        name="gather_project",
    )(conved, weight, tokens, tails, gain, taps, putting, slots)


def scatter_kernel(
    rows, att_ref, w_ref, served_ref, place_ref, out_ref, dec_out_ref,
    part, far, near, far_last, near_last, landing, dec_wide, dec_ref, dec_in,
    send_sem, far_sem, near_sem, dec_send, dec_recv, swap_send, swap_recv,
):
    me, mx, my = plane_position()
    peers = [lax.rem(me + k, 16) for k in range(1, 16)]
    barrier, callers = greet(peers)
    sent = []

    def send(half, along_first, step, source, target_ref, sem):
        copy = pltpu.make_async_remote_copy(
            src_ref=source,
            dst_ref=target_ref,
            send_sem=send_sem.at[len(sent)],
            recv_sem=sem,
            device_id={
                "head": block_at(half, step if along_first else 0, 0 if along_first else step, mx, my)
            },
            device_id_type=MESH,
        )
        copy.start()
        sent.append(copy)

    def arrived(place, sem):
        pltpu.make_async_remote_copy(
            src_ref=place,
            dst_ref=place,
            send_sem=send_sem.at[0],
            recv_sem=sem,
            device_id={"head": block_at(0, 1, 0, mx, my)},
            device_id_type=MESH,
        ).wait_recv()

    def project(dx, dy):
        block = block_at(0, dx, dy, mx, my)
        value = att_ref[pl.ds(pl.multiple_of(block * rows, rows), rows), :]
        product = jnp.dot(value, w_ref[...], preferred_element_type=jnp.float32)
        part[block] = product.astype(jnp.bfloat16)

    def piece(half, first, second, quarter=None):
        return block_at(half, first, second, mx, my), half_rows(half, quarter, rows)

    def wide(value):
        return value.astype(jnp.float32)

    def send_far(half, first):
        for quarter, step in ((0, -1), (1, 1)):
            block, span = piece(half, first, 2, quarter)
            slot = half * SIDE + first
            send(half, False, step, part.at[block, span], far.at[slot, quarter], far_sem.at[slot, quarter])

    order = (2, 1, 3, 0)
    for first in order:
        for dx, dy in sorted({(first, 2), (2, first)}):
            project(dx, dy)
    for dx, dy in ((1, 1), (1, 3), (3, 1), (3, 3), (0, 1), (1, 0)):
        project(dx, dy)
    pl.semaphore_wait(barrier, callers)
    for first in order:
        for half in (0, 1):
            send_far(half, first)
    swap_start(served_ref, landing, swap_send, swap_recv)
    for dx, dy in ((3, 0), (0, 3), (0, 0)):
        project(dx, dy)
    for first in order:
        for half in (0, 1):
            slot = half * SIDE + first
            for quarter, step in ((0, -1), (1, 1)):
                arrived(far.at[slot, quarter], far_sem.at[slot, quarter])
                block, span = piece(half, first, step, quarter)
                part[block, span, :] = (wide(part[block, span, :]) + wide(far[slot, quarter])).astype(jnp.bfloat16)
                block, span = piece(half, first, step)
                send(half, False, step, part.at[block, span], near.at[slot, quarter], near_sem.at[slot, quarter])
    swap_finish(served_ref, landing, swap_send, swap_recv)
    groups, item_rows, lanes = landing.shape
    returned = landing[...].reshape(groups * item_rows, lanes).astype(jnp.bfloat16)
    dec_att = jnp.dot(place_ref[...], returned, preferred_element_type=jnp.float32)
    dec_att = dec_att.astype(jnp.bfloat16)[:, : w_ref.shape[0]]
    dec_part = jnp.dot(dec_att, w_ref[...], preferred_element_type=jnp.float32)
    dec_wide[...] = jnp.zeros(dec_wide.shape, jnp.float32)
    per_peer = dec_part.shape[0] // 16
    for chunk in range(dec_part.shape[1] // lanes):
        for row in range(per_peer):
            dec_wide[:, chunk * per_peer + row, :] = dec_part[
                row * 16 : row * 16 + 16, chunk * lanes : (chunk + 1) * lanes
            ]
    dec_ref[...] = dec_wide[...].astype(jnp.bfloat16)
    dec_copies = []
    for k, peer in enumerate(peers):
        copy = pltpu.make_async_remote_copy(
            src_ref=dec_ref.at[peer],
            dst_ref=dec_in.at[k],
            send_sem=dec_send.at[k],
            recv_sem=dec_recv.at[k],
            device_id={"head": peer},
            device_id_type=MESH,
        )
        copy.start()
        dec_copies.append(copy)
    for first in order:
        for half in (0, 1):
            slot = half * SIDE + first
            for quarter in (0, 1):
                arrived(near.at[slot, quarter], near_sem.at[slot, quarter])
            block, span = piece(half, first, 0)
            if first == 0:
                continue
            total = wide(part[block, span, :]) + wide(near[slot, 0]) + wide(near[slot, 1])
            part[block, span, :] = total.astype(jnp.bfloat16)
            if first == 2:
                for quarter, step in ((0, -1), (1, 1)):
                    block, span = piece(half, 2, 0, quarter)
                    send(half, True, step, part.at[block, span], far_last.at[half, quarter], far_sem.at[8 + half, quarter])
            else:
                quarter, step = (1, 1) if first == 1 else (0, -1)
                arrived(far_last.at[half, quarter], far_sem.at[8 + half, quarter])
                inner, inner_span = piece(half, step, 0, quarter)
                part[inner, inner_span, :] = (
                    wide(part[inner, inner_span, :]) + wide(far_last[half, quarter])
                ).astype(jnp.bfloat16)
                send(half, True, step, part.at[block, span], near_last.at[half, quarter], near_sem.at[8 + half, quarter])
    dec_total = wide(dec_ref[me])
    for k, copy in enumerate(dec_copies):
        copy.wait_recv()
        dec_total = dec_total + wide(dec_in[k])
    dec_out_ref[...] = dec_total.astype(jnp.bfloat16)
    for half in (0, 1):
        block, span = piece(half, 0, 0)
        total = wide(part[block, span, :]) + wide(near[half * SIDE, 0]) + wide(near[half * SIDE, 1])
        for quarter in (0, 1):
            arrived(near_last.at[half, quarter], near_sem.at[8 + half, quarter])
            total = total + wide(near_last[half, quarter])
        out_ref[span, :] = total.astype(jnp.bfloat16)
    for copy in sent:
        copy.wait_send()
    for copy in dec_copies:
        copy.wait_send()


def project_scatter(attended, weight, served, placing):
    rows = attended.shape[0] // 16
    width = weight.shape[1]
    lanes = served.shape[2]
    dec_rows = -(-placing.shape[0] // 16 * width // lanes // 16) * 16
    whole = pl.BlockSpec(memory_space=pltpu.VMEM)
    return pl.pallas_call(
        functools.partial(scatter_kernel, rows),
        out_shape=(
            jax.ShapeDtypeStruct((rows, width), jnp.bfloat16),
            jax.ShapeDtypeStruct((dec_rows, lanes), jnp.bfloat16),
        ),
        in_specs=[whole, whole, whole, whole],
        out_specs=(whole, whole),
        scratch_shapes=[
            pltpu.VMEM((16, rows, width), jnp.bfloat16),
            pltpu.VMEM((8, 2, rows // 4, width), jnp.bfloat16),
            pltpu.VMEM((8, 2, rows // 2, width), jnp.bfloat16),
            pltpu.VMEM((2, 2, rows // 4, width), jnp.bfloat16),
            pltpu.VMEM((2, 2, rows // 2, width), jnp.bfloat16),
            pltpu.VMEM(served.shape, served.dtype),
            pltpu.VMEM((16, dec_rows, lanes), jnp.float32),
            pltpu.VMEM((16, dec_rows, lanes), jnp.bfloat16),
            pltpu.VMEM((15, dec_rows, lanes), jnp.bfloat16),
            pltpu.SemaphoreType.DMA((40,)),
            pltpu.SemaphoreType.DMA((10, 2)),
            pltpu.SemaphoreType.DMA((10, 2)),
            pltpu.SemaphoreType.DMA((15,)),
            pltpu.SemaphoreType.DMA((15,)),
            pltpu.SemaphoreType.DMA((served.shape[0],)),
            pltpu.SemaphoreType.DMA((served.shape[0],)),
        ],
        compiler_params=pltpu.CompilerParams(
            collective_id=1, has_side_effects=True, vmem_limit_bytes=40 * 2**20
        ),
        name="project_scatter",
    )(attended, weight, served, placing)


def from_behind(array, axis, by):
    peers = lax.axis_size(axis)
    pairs = [(i, i + by) for i in range(peers) if 0 <= i + by < peers]
    return lax.ppermute(array, axis, pairs)


def rms_rows(values, gain):
    values = values.astype(jnp.float32)
    factor = lax.rsqrt(jnp.mean(values * values, axis=-1, keepdims=True) + 1e-05)
    return values * factor * gain


def features(vectors):
    breadth = vectors.shape[-1]
    linear = vectors / math.sqrt(math.sqrt(breadth))
    index = jnp.arange(breadth * breadth)[None, :]
    which = jnp.arange(breadth)[:, None]
    slow = (index // breadth == which).astype(jnp.bfloat16)
    fast = (index % breadth == which).astype(jnp.bfloat16)
    exact = vectors.astype(jnp.bfloat16)
    outer = jnp.dot(exact, slow, preferred_element_type=jnp.float32) * jnp.dot(
        exact, fast, preferred_element_type=jnp.float32
    )
    outer = outer / math.sqrt(2.0 * breadth)
    ones = jnp.ones(vectors.shape[:-1] + (1,), vectors.dtype)
    return jnp.concatenate([ones, linear, outer], axis=-1)


def convolve(tail, normed, conv_taps):
    joined = jnp.concatenate([tail, normed], axis=-2).astype(jnp.float32)
    span_rows = normed.shape[-2]
    total = conv_taps[0] * joined[..., 0:span_rows, :]
    total = total + conv_taps[1] * joined[..., 1 : span_rows + 1, :]
    total = total + conv_taps[2] * joined[..., 2 : span_rows + 2, :]
    return total.astype(jnp.bfloat16)


def decode_items(items, slot_items, cache_own, out_gain, head_count):
    item_count = items.shape[0]
    shaped = items.reshape(item_count, head_count, 2 * F + DH).astype(jnp.float32)
    queries = shaped[:, :, :F]
    key_feats = shaped[:, :, F : 2 * F]
    values = shaped[:, :, 2 * F :]
    slot_total = cache_own.shape[0]
    table = jnp.einsum(
        "nhp,shdp->nshd", features(queries), cache_own, precision=lax.Precision.HIGH
    )
    picker = (slot_items[:, None] == jnp.arange(slot_total)[None, :]).astype(jnp.float32)
    carried = jnp.einsum("ns,nshd->nhd", picker, table, precision=lax.Precision.HIGHEST)
    inner = jnp.sum(queries * key_feats, axis=-1) / math.sqrt(F)
    own_term = (1.0 + inner + 0.5 * inner * inner)[..., None] * values
    attended = rms_rows(carried + own_term, out_gain.reshape(head_count, DH))
    return attended.astype(jnp.bfloat16).reshape(item_count, head_count * DH)


def local(
    stretch_tokens,
    stretch_tail,
    decode_tokens,
    decode_tail,
    norm_gain,
    conv_taps,
    qkv_weight,
    out_gain,
    out_weight,
    state_cache,
    stretch_len,
    stretch_slot,
    decode_slot,
    decode_owner,
):
    head_count = qkv_weight.shape[1]
    block_width = qkv_weight.shape[2]
    rows_own = stretch_tokens.shape[1]
    w_flat = qkv_weight.reshape(D, head_count * block_width)
    gains = out_gain.reshape(head_count, DH)
    normed = rms_rows(stretch_tokens[0], norm_gain).astype(jnp.bfloat16)
    rim_rows = from_behind(normed[rows_own - 2 :], "head", 1)
    first_dev = lax.axis_index("head") == 0
    rim_rows = jnp.where(first_dev, stretch_tail[0], rim_rows)
    conved = convolve(rim_rows, normed, conv_taps)
    owners = decode_owner[0, :, 0]
    slots_here = decode_slot[0]
    groups = lax.axis_size("tok")
    capacity = max(2, 2 * DEC // groups)
    earlier = jnp.arange(DEC)[None, :] < jnp.arange(DEC)[:, None]
    same_owner = owners[None, :] == owners[:, None]
    rank_in = jnp.sum(earlier & same_owner, axis=1)
    spots = owners * 8 + rank_in
    lines = jnp.arange(groups * 8)
    gathering = (lines[:, None] == spots[None, :]).astype(jnp.bfloat16)
    named = lines[:, None] == spots[None, :] + capacity
    slot_column = jnp.sum(jnp.where(named, slots_here[None, :], 0), axis=1, keepdims=True)
    grouped, items = gather_project(
        conved, w_flat, decode_tokens[0], decode_tail[0].reshape(DEC, 2 * D), norm_gain,
        conv_taps, gathering, slot_column.astype(jnp.float32),
    )
    grouped = grouped.reshape(STRETCH, head_count, block_width)
    queries = grouped[:, :, :F]
    key_feats = grouped[:, :, F : 2 * F]
    values = grouped[:, :, 2 * F :]
    length = stretch_len[0]
    positions = jnp.arange(STRETCH)
    valid_rows = positions < length
    state_old = lax.dynamic_index_in_dim(state_cache[0], stretch_slot[0], 0, keepdims=False)
    carried = jnp.einsum(
        "ihp,hdp->ihd",
        features(queries.astype(jnp.float32)),
        state_old,
        precision=lax.Precision.HIGH,
    )
    block_rows = min(512, STRETCH)
    pieces = []
    for anchor in range(0, STRETCH, block_rows):
        finish = anchor + block_rows
        inner = jnp.einsum(
            "ihf,jhf->hij",
            queries[anchor:finish],
            key_feats[:finish],
            preferred_element_type=jnp.float32,
        ) / math.sqrt(F)
        weights = 1.0 + inner + 0.5 * inner * inner
        allowed = (positions[None, :finish] <= positions[anchor:finish, None]) & valid_rows[
            None, :finish
        ]
        weights = jnp.where(allowed[None], weights, 0.0).astype(jnp.bfloat16)
        pieces.append(
            jnp.einsum("hij,jhd->ihd", weights, values[:finish], preferred_element_type=jnp.float32)
        )
    local_sum = jnp.concatenate(pieces, axis=0)
    attended = rms_rows(carried + local_sum, gains)
    attended = (
        jnp.where(valid_rows[:, None, None], attended, 0.0)
        .astype(jnp.bfloat16)
        .reshape(STRETCH, head_count * DH)
    )
    key_phi = jnp.where(
        valid_rows[:, None, None], features(key_feats.astype(jnp.float32)), 0.0
    ).astype(jnp.bfloat16)
    state_next = state_old + jnp.einsum(
        "jhd,jhp->hdp", values, key_phi, preferred_element_type=jnp.float32
    )
    wide = head_count * block_width
    item_rows = items[:, :capacity, :wide].reshape(groups * capacity, wide)
    item_slots = items[:, capacity : 2 * capacity, 0].reshape(groups * capacity)
    served = decode_items(
        item_rows, item_slots.astype(jnp.int32), state_cache[0], out_gain, head_count
    )
    served = served.astype(jnp.float32).reshape(groups, capacity, head_count * DH)
    served = jnp.pad(served, ((0, 0), (0, 8 - capacity), (0, 128 - head_count * DH)))
    heads = lax.axis_size("head")
    per_head = DEC // heads
    returns = spots.reshape(heads, per_head).T.reshape(DEC)
    putting = (returns[:, None] == jnp.arange(groups * 8)[None, :]).astype(jnp.bfloat16)
    stretch_out, dec_sum = project_scatter(attended, out_weight, served, putting)
    dec_sum = dec_sum[: per_head * D // 128].reshape(D // 128, per_head, 128)
    decode_out = jnp.transpose(dec_sum, (1, 0, 2)).reshape(per_head, D)
    return (stretch_out[None], decode_out[None], state_next[None])


def solution(mesh):
    in_specs = (
        P("tok", "head", None),
        P("tok", None, None),
        P("tok", None, None),
        P("tok", None, None, None),
        P(),
        P(),
        P(None, "head", None),
        P("head"),
        P("head", None),
        P("tok", None, "head", None, None),
        P("tok"),
        P("tok"),
        P("tok", None),
        P("tok", None, None),
    )
    out_specs = (P("tok", "head", None), P("tok", "head", None), P("tok", "head", None, None))
    return jax.shard_map(local, mesh=mesh, in_specs=in_specs, out_specs=out_specs, check_vma=False)
```
